512 devices in a mesh: gx: 32 (over y, x), gy: 16 (over z, core).
Axes of the slice: x: 4, y: 8, z: 8, core: 2. Of those that a mesh axis runs over, the one named last changes fastest.
Arguments:
- spectra: float32 [64, 4, 33, 4, 2048], P('gx', None, None, None, 'gy'), may hold values from 0.05 to 2
- collection: float32 [4, 33, 561], replicated, may hold values from -0.125 to 0.125
- growth_rate: float32 [4, 33], replicated, may hold values from 0.1 to 1
- fall_speed: float32 [4, 33], replicated, may hold values from 0.05 to 0.9
- supersaturation: float32 [64, 4, 2048], P('gx', None, 'gy'), may hold values from -0.4 to 0.4
- courant: float32 [64, 4, 2048], P('gx', None, 'gy'), may hold values from -0.8 to 0.8
- cloudy: int32 [64, 2048], P('gx', 'gy'), may hold values from 0 to 1, as said below
Outputs:
- spectra_out: float32 [64, 4, 33, 4, 2048], P('gx', None, None, None, 'gy')
The draws below stay inside these ranges and needn't reach their ends.
Inputs may be any that keep to these rules, and one draw needn't show every extreme that they name: A block is the 128 columns of one x-row that lie on one device; each device holds 2 blocks, and a block is cloudy if any of its entries is 1. In every aligned run of 8 devices along gx with one gy index at most 8 blocks are cloudy; in every draw some run has exactly that many, and some device has all 2 of its blocks cloudy.
All inputs are finite; a program needn't handle non-finite values.
Results may differ from the reference program's by a relative error of at most 0.0003.
Values sent between devices are 32-bit elements; how exact they have to be, the bound alone decides.
No kernel may reach another device: no remote copies, remote signals or barrier semaphores. Data moves between devices by JAX's collectives and lax.ppermute only.
A program may use at most 64 MiB of HBM per device.

```python
import math
import jax
import jax.numpy as jnp
from jax import lax

TYPES = 4
BINS = 33
LEV = 4
CY = 128
BLK_DEV = 2
SUB = 2
GROUP = 8
CAP = 1
PAIRS = 561
NX = 64
NY = 2048


def draw_cloudy(key, part):
    rows_group = BLK_DEV * GROUP
    x_groups = NX // rows_group
    y_blocks = NY // CY
    group_count = x_groups * y_blocks
    keys = jax.random.split(jax.random.fold_in(key, 7), 6)
    counts = jax.random.randint(keys[0], (group_count,), BLK_DEV, GROUP * CAP + 1)
    full_group = jax.random.randint(keys[1], (), 0, group_count)
    counts = jnp.where(jnp.arange(group_count) == full_group, GROUP * CAP, counts)
    favored = jax.random.randint(keys[2], (group_count, 1), 0, GROUP)
    slot_ids = jnp.arange(rows_group, dtype=jnp.int32)
    scores = jax.random.randint(keys[3], (group_count, rows_group), 0, 1 << 20) * rows_group + slot_ids
    scores = scores + jnp.where(slot_ids[None, :] // BLK_DEV == favored, 1 << 28, 0)
    ordering = jnp.argsort(-scores, axis=1)
    ranking = jnp.argsort(ordering, axis=1)
    block_on = (ranking < counts[:, None]).astype(jnp.int32)
    block_on = block_on.reshape(x_groups, y_blocks, rows_group).transpose(0, 2, 1).reshape(NX, y_blocks, 1)
    column_bits = jax.random.randint(keys[4], (NX, y_blocks, CY), 0, 4) > 0
    forced = jax.random.randint(keys[5], (NX, y_blocks, 1), 0, CY)
    column_on = (column_bits | (jnp.arange(CY)[None, None, :] == forced)).astype(jnp.int32)
    return (block_on * column_on).reshape(NX, NY)


def steps_of(stream_key, dims, cuts, smallest, high):
    loudness = 1.0
    for axis_at, blocks in cuts:
        draws = jax.random.uniform(jax.random.fold_in(jax.random.fold_in(stream_key, 6), axis_at), (blocks,), jnp.float32, smallest / len(cuts), high / len(cuts))
        loudness = loudness * jnp.repeat(jnp.exp(draws), dims[axis_at] // blocks).reshape((-1,) + (1,) * (len(dims) - 1 - axis_at))
    return loudness


def noise(stream_key, extent, deviation, bound, kind=jnp.bfloat16):
    return jnp.clip(deviation * jax.random.normal(stream_key, extent, jnp.float32), -bound, bound).astype(kind)


def setup_inputs(seed: int = 0) -> dict:
    key_list = jax.random.split(jax.random.key(seed), 8)
    spectra = jnp.clip(jnp.exp(math.log(2.0) - 3.6888794 * jax.random.uniform(key_list[0], (NX, TYPES, BINS, LEV, NY), jnp.float32) ** steps_of(key_list[0], (NX, TYPES, BINS, LEV, NY), ((0, 32), (4, 16)), -0.2, 0.2)), 0.05, 2.0)
    collection = noise(key_list[1], (TYPES, BINS, PAIRS), (4 * PAIRS) ** -0.5, 0.125, jnp.float32)
    growth_rate = jnp.clip(jnp.exp(jax.random.uniform(key_list[2], (TYPES, BINS), jnp.float32, math.log(0.1), math.log(1.0))), 0.1, 1.0)
    fall_speed = jnp.clip(jnp.exp(jax.random.uniform(key_list[3], (TYPES, BINS), jnp.float32, math.log(0.05), math.log(0.9))), 0.05, 0.9)
    supersaturation = jnp.clip(jax.random.uniform(key_list[4], (NX, LEV, NY), jnp.float32, -0.4, 0.4) * steps_of(key_list[4], (NX, LEV, NY), ((0, 32), (2, 16)), -0.4, 0.0), -0.4, 0.4)
    courant = jnp.clip(jax.random.uniform(key_list[5], (NX, LEV, NY), jnp.float32, -0.8, 0.8) * steps_of(key_list[5], (NX, LEV, NY), ((0, 32), (2, 16)), -0.4, 0.0), -0.8, 0.8)
    cloudy = draw_cloudy(jax.random.fold_in(key_list[7], 71), 0)
    return {"spectra": spectra, "collection": collection, "growth_rate": growth_rate, "fall_speed": fall_speed, "supersaturation": supersaturation, "courant": courant, "cloudy": cloudy}


precise_mode = lax.Precision.HIGHEST


def pair_products(matrix):
    pieces = [matrix[first:first + 1] * matrix[first:] for first in range(matrix.shape[0])]
    return jnp.concatenate(pieces, axis=0)


def condense(block, saturation, growth_rate):
    rising = jnp.maximum(saturation, 0.0)
    falling = jnp.maximum(-saturation, 0.0)
    transfer = growth_rate[:, :, None, None] * block
    upward = rising * transfer
    upward = jnp.concatenate([upward[:, :-1], jnp.zeros_like(upward[:, :1])], axis=1)
    downward = falling * transfer
    arrive_up = jnp.concatenate([jnp.zeros_like(upward[:, :1]), upward[:, :-1]], axis=1)
    arrive_down = jnp.concatenate([downward[:, 1:], jnp.zeros_like(downward[:, :1])], axis=1)
    return block - upward - downward + arrive_up + arrive_down


def collide(block, collection):
    results = []
    for species in range(block.shape[0]):
        matrix = block[species].reshape(block.shape[1], -1)
        gained = jnp.dot(collection[species], pair_products(matrix), precision=precise_mode, preferred_element_type=jnp.float32)
        results.append(matrix + gained)
    return jnp.stack(results).reshape(block.shape)


def micro_block(block, saturation, cloudy_row, growth_rate, collection):
    grown = condense(block, saturation, growth_rate)
    for substep in range(SUB):
        grown = collide(grown, collection)
    return jnp.where(cloudy_row > 0, grown, block)


def sediment(block, fall_speed):
    above = jnp.concatenate([block[..., 1:, :], jnp.zeros_like(block[..., :1, :])], axis=-2)
    return block + fall_speed[:, :, None, None] * (above - block)


def advect(extended, courant_ext):
    columns = extended.shape[-1] - 4
    face_courant = 0.5 * (courant_ext[..., 1:columns + 2] + courant_ext[..., 2:columns + 3])
    minus_one = extended[..., 0:columns + 1]
    centre = extended[..., 1:columns + 2]
    plus_one = extended[..., 2:columns + 3]
    plus_two = extended[..., 3:columns + 4]
    central = (7.0 * (plus_one + centre) - (plus_two + minus_one)) / 12.0
    upwind = ((plus_two - minus_one) - 3.0 * (plus_one - centre)) / 12.0
    fluxes = face_courant * central - jnp.abs(face_courant) * upwind
    return extended[..., 2:columns + 2] - (fluxes[..., 1:] - fluxes[..., :-1])


def reference(spectra, collection, growth_rate, fall_speed, supersaturation, courant, cloudy):
    def one_row(pieces):
        block, saturation, wind_row, cloudy_row = pieces
        wetted = micro_block(block, saturation, cloudy_row, growth_rate, collection)
        settled = sediment(wetted, fall_speed)
        extended = jnp.concatenate([settled[..., -2:], settled, settled[..., :2]], axis=-1)
        wind_ext = jnp.concatenate([wind_row[..., -2:], wind_row, wind_row[..., :2]], axis=-1)
        return advect(extended, wind_ext)
    return lax.map(one_row, (spectra, supersaturation, courant, cloudy))
```

```python
import jax
import jax.numpy as jnp
from jax import lax
from jax.experimental import pallas as pl
from jax.experimental.pallas import tpu as pltpu
from jax.sharding import PartitionSpec as P

TYPES = 4
BINS = 33
LEV = 4
BLK = 2
SUB = 2
COLS = 128
ROWS = BLK * TYPES * BINS * LEV
PAIRS = BINS * (BINS + 1) // 2
HALF = 512
TAIL = 64
KDIM = HALF + 2 * TAIL
MROWS = 80
F32 = jnp.float32
BF16 = jnp.bfloat16


def iota(shape, axis):
    return lax.broadcasted_iota(jnp.int32, shape, axis)


def split(x):
    high = x.astype(BF16)
    low = (x - high.astype(F32)).astype(BF16)
    return high, low


def block_row(t, b):
    return (b * TYPES + t) * BINS * LEV


def pair_of_column(col):
    tail = jnp.where(col >= HALF + TAIL, col - TAIL, col)
    first = jnp.where(col < HALF, col & 31, jnp.where(tail < 528, tail - HALF, tail - 528))
    second = jnp.where(
        col < HALF, (first + (col >> 5)) & 31, jnp.where(tail < 528, first + 16, BINS - 1)
    )
    low = jnp.minimum(first, second)
    high = jnp.maximum(first, second)
    pair = low * BINS - ((low * (low - 1)) >> 1) + (high - low)
    return jnp.where(tail > 560, -1, pair)


def edge_kernel(spec, sat, wind, cloudy, coll, growth, fall, edge, lhs, coef, raw, parts):
    lane = iota((1, COLS), 1)
    owner = ((lane + 2) & 127) >> 2
    row8 = iota((8, COLS), 0)
    main = [jnp.zeros((8, COLS), F32) for _ in range(4)]
    last = jnp.zeros((8, COLS), F32)
    for b in range(BLK):
        cloud_row = cloudy[b : b + 1, :].astype(F32)
        for l in range(LEV):
            extra = jnp.where(
                row8 == 1,
                sat[b * LEV + l : b * LEV + l + 1, :],
                jnp.where(row8 == 2, wind[b * LEV + l : b * LEV + l + 1, :], cloud_row),
            )
            for t in range(TYPES):
                spot = (t * BLK + b) * LEV + l
                mine = owner == spot
                start = block_row(t, b) + l
                for q in range(4):
                    piece = spec[pl.ds(start + 32 * q, 8, stride=LEV), :]
                    main[q] = jnp.where(mine, pltpu.roll(piece, 4 * spot, 1), main[q])
                piece = jnp.where(row8 == 0, spec[start + 128 : start + 129, :], extra)
                last = jnp.where(mine, pltpu.roll(piece, 4 * spot, 1), last)
    for q in range(4):
        edge[8 * q : 8 * q + 8, :] = main[q]
    edge[32:40, :] = last

    stacked = jnp.concatenate(
        [
            jnp.concatenate([growth[...], fall[...]], axis=0),
            jnp.zeros((COLS - 2 * TYPES, BINS), F32),
        ],
        axis=0,
    )
    stacked = jnp.concatenate([stacked, jnp.zeros((COLS, COLS - BINS), F32)], axis=1)
    turned = jnp.transpose(stacked)[0:40, :]
    for n in range(2 * TYPES):
        coef[n] = jnp.broadcast_to(turned[:, n : n + 1], (40, COLS))

    raw[...] = jnp.zeros(raw.shape, F32)
    for n in range(KDIM // COLS):
        width = min(COLS, PAIRS - COLS * n)
        for k in range(BINS):
            raw[n, TYPES * k : TYPES * k + TYPES, 0:width] = coll[k, :, COLS * n : COLS * n + width]
    parts[...] = jnp.zeros(parts.shape, BF16)
    for t in range(TYPES):
        for n in range(KDIM // COLS):
            rows = raw[n, pl.ds(t, 40, stride=TYPES), :]
            both = jnp.concatenate(split(rows), axis=0)
            parts[MROWS * t : MROWS * t + MROWS, COLS * n : COLS * n + COLS] = both
    wanted = pair_of_column(iota((1, KDIM), 1))
    chosen = jnp.where(iota((KDIM, KDIM), 0) == wanted, 1.0, 0.0).astype(BF16)
    lhs[...] = jnp.dot(parts[...], chosen, preferred_element_type=F32).astype(BF16)


def condense(main, top, sat, rate_main, rate_top):
    rising = jnp.maximum(sat, 0.0)
    falling = jnp.maximum(-sat, 0.0)
    transfer = rate_main * main
    up = rising * transfer
    down = falling * transfer
    down_top = falling * (rate_top * top)
    arrive_up = jnp.concatenate([jnp.zeros_like(top), up[:-1]], axis=0)
    arrive_down = jnp.concatenate([down[1:], down_top], axis=0)
    new_main = main - up - down + arrive_up + arrive_down
    new_top = top - down_top + up[-1:]
    return new_main, new_top


def store_pairs(main, top, turn, high_ref, low_ref, tail_ref, lanes):
    turn[0:32, :] = main
    turn[32:48, :] = main[0:16]
    for d in range(16):
        other = main if d == 0 else turn[d : d + 32, :]
        high, low = split(main * other)
        high_ref[32 * d : 32 * d + 32, lanes] = high
        low_ref[32 * d : 32 * d + 32, lanes] = low
    square = jnp.where(iota((16, COLS), 0) == 0, top * top, 0.0)
    rest = jnp.concatenate([main[0:16] * main[16:32], main * top, square], axis=0)
    high, low = split(rest)
    tail_ref[0:TAIL, lanes] = high
    tail_ref[TAIL : 2 * TAIL, lanes] = low


def collect(lhs, high_ref, low_ref, tail_ref):
    def part(left, right):
        return jnp.dot(left, right, preferred_element_type=F32)

    return (
        part(lhs[:, 0:HALF], high_ref[...])
        + part(lhs[:, 0:HALF], low_ref[...])
        + part(lhs[:, HALF:KDIM], tail_ref[...])
    )


def main_kernel(spec, sat, cloudy, lhs, coef, settled, turn, high_ref, low_ref, tail_ref):
    def one(n, carry):
        t = n >> 1
        b = n & 1
        start = block_row(t, b)
        left = lhs[pl.ds(pl.multiple_of(t * MROWS, 16), MROWS), :]
        rate = coef[t]
        speed = coef[TYPES + t]
        wet = cloudy[pl.ds(b, 1), :] > 0
        before = []
        state = []
        for l in range(LEV):
            main = spec[pl.ds(start + l, 32, stride=LEV), :]
            top = spec[pl.ds(start + 128 + l, 1), :]
            before.append((main, top))
            row = sat[pl.ds(b * LEV + l, 1), :]
            state.append(condense(main, top, row, rate[0:32], rate[32:33]))
        for step in range(SUB):
            for half in range(2):
                at = 2 * step + half
                for k in range(2):
                    l = 2 * half + k
                    store_pairs(
                        *state[l],
                        turn.at[LEV * step + l],
                        high_ref.at[at],
                        low_ref.at[at],
                        tail_ref.at[at],
                        slice(COLS * k, COLS * k + COLS),
                    )
                gain = collect(left, high_ref.at[at], low_ref.at[at], tail_ref.at[at])
                for k in range(2):
                    l = 2 * half + k
                    mine = gain[:, COLS * k : COLS * k + COLS]
                    main, top = state[l]
                    state[l] = (
                        main + (mine[0:32] + mine[40:72]),
                        top + (mine[32:33] + mine[72:73]),
                    )
        above = None
        for l in reversed(range(LEV)):
            main = jnp.where(wet, state[l][0], before[l][0])
            top = jnp.where(wet, state[l][1], before[l][1])
            over = (jnp.zeros_like(main), jnp.zeros_like(top)) if above is None else above
            settled[n, l, 0:32, :] = main + speed[0:32] * (over[0] - main)
            settled[n, l, 32:33, :] = top + speed[32:33] * (over[1] - top)
            above = (main, top)
        return carry

    lax.fori_loop(0, BLK * TYPES, one, 0)


def finish_kernel(settled, from_left, from_right, wind, lhs, coef, out, turn, high_ref, low_ref, tail_ref):
    lane = iota((1, COLS), 1)
    owner = ((lane + 2) & 127) >> 2
    kind = owner >> 3
    halo = jnp.where((lane & 3) < 2, from_right[...], from_left[...])

    def by_type(pieces):
        value = pieces[0]
        for t in range(1, TYPES):
            value = jnp.where(kind == t, pieces[t], value)
        return value

    rate = by_type([coef[t] for t in range(TYPES)])
    speed = by_type([coef[TYPES + t] for t in range(TYPES)])
    main = halo[0:32]
    top = halo[32:33]
    wet = halo[35:36] > 0
    state = condense(main, top, halo[33:34], rate[0:32], rate[32:33])
    for step in range(SUB):
        store_pairs(
            *state,
            turn.at[step],
            high_ref.at[step],
            low_ref.at[step],
            tail_ref.at[step],
            slice(0, COLS),
        )
        gain = collect(lhs[...], high_ref.at[step], low_ref.at[step], tail_ref.at[step])
        mine = by_type([gain[MROWS * t : MROWS * t + MROWS] for t in range(TYPES)])
        state = (
            state[0] + (mine[0:32] + mine[40:72]),
            state[1] + (mine[32:33] + mine[72:73]),
        )
    highest = (owner & 3) == LEV - 1

    def settle(value, speed):
        above = jnp.where(highest, 0.0, pltpu.roll(value, COLS - 4, 1))
        return value + speed * (above - value)

    edge = jnp.concatenate(
        [
            settle(jnp.where(wet, state[0], main), speed[0:32]),
            settle(jnp.broadcast_to(jnp.where(wet, state[1], top), (8, COLS)), speed[32:40]),
        ],
        axis=0,
    )
    edge_wind = jnp.broadcast_to(halo[34:35], (8, COLS))

    def shifted(value, ghost, by):
        if by > 0:
            return pltpu.roll(jnp.where(lane < by, ghost, value), COLS - by, 1)
        return pltpu.roll(jnp.where(lane >= COLS + by, ghost, value), -by, 1)

    for b in range(BLK):
        for l in range(LEV):
            ghost = pltpu.roll(edge_wind, (COLS - 4 * (b * LEV + l)) % COLS, 1)
            own = jnp.broadcast_to(wind[b * LEV + l : b * LEV + l + 1, :], (8, COLS))
            right = (own + shifted(own, ghost, 1)) * (0.5 / 12.0)
            left = (own + shifted(own, ghost, -1)) * (0.5 / 12.0)
            right_abs = jnp.abs(right)
            left_abs = jnp.abs(left)
            w_p2 = (right + right_abs)[0:1]
            w_p1 = (-(7.0 * right + 3.0 * right_abs) - (left + left_abs))[0:1]
            w_0 = (1.0 - (7.0 * right - 3.0 * right_abs) + (7.0 * left + 3.0 * left_abs))[0:1]
            w_m1 = ((right - right_abs) + (7.0 * left - 3.0 * left_abs))[0:1]
            w_m2 = (left_abs - left)[0:1]
            for t in range(TYPES):
                n = t * BLK + b
                x = settled[n, l]
                g = pltpu.roll(edge, (COLS - 4 * (n * LEV + l)) % COLS, 1)
                y = (
                    w_0 * x
                    + w_p1 * shifted(x, g, 1)
                    + w_m1 * shifted(x, g, -1)
                    + w_p2 * shifted(x, g, 2)
                    + w_m2 * shifted(x, g, -2)
                )
                start = block_row(t, b) + l
                for q in range(4):
                    out[pl.ds(start + 32 * q, 8, stride=LEV), :] = y[8 * q : 8 * q + 8]
                out[start + 128 : start + 129, :] = y[32:33]


def vmem(count):
    return [pl.BlockSpec(memory_space=pltpu.VMEM)] * count


def body(spectra, collection, growth_rate, fall_speed, supersaturation, courant, cloudy):
    spec = spectra.reshape(ROWS, COLS)
    sat = supersaturation.reshape(BLK * LEV, COLS)
    wind = courant.reshape(BLK * LEV, COLS)
    coll = jnp.transpose(collection, (1, 0, 2))
    edge, lhs, coef = pl.pallas_call(
        edge_kernel,
        out_shape=(
            jax.ShapeDtypeStruct((40, COLS), F32),
            jax.ShapeDtypeStruct((TYPES * MROWS, KDIM), BF16),
            jax.ShapeDtypeStruct((2 * TYPES, 40, COLS), F32),
        ),
        in_specs=vmem(7),
        out_specs=tuple(vmem(3)),
        scratch_shapes=[
            pltpu.VMEM((KDIM // COLS, TYPES * 40, COLS), F32),
            pltpu.VMEM((TYPES * MROWS, KDIM), BF16),
        ],
        name="edges",
    )(spec, sat, wind, cloudy, coll, growth_rate, fall_speed)
    count = lax.axis_size("gy")
    up = [(i, (i + 1) % count) for i in range(count)]
    down = [(j, i) for i, j in up]
    from_left = lax.ppermute(edge, "gy", up)
    from_right = lax.ppermute(edge, "gy", down)
    settled = pl.pallas_call(
        main_kernel,
        out_shape=jax.ShapeDtypeStruct((BLK * TYPES, LEV, 40, COLS), F32),
        in_specs=vmem(5),
        out_specs=vmem(1)[0],
        scratch_shapes=[
            pltpu.VMEM((SUB * LEV, 48, COLS), F32),
            pltpu.VMEM((2 * SUB, HALF, 2 * COLS), BF16),
            pltpu.VMEM((2 * SUB, HALF, 2 * COLS), BF16),
            pltpu.VMEM((2 * SUB, 2 * TAIL, 2 * COLS), BF16),
        ],
        name="blocks",
    )(spec, sat, cloudy, lhs, coef)
    out = pl.pallas_call(
        finish_kernel,
        out_shape=jax.ShapeDtypeStruct((ROWS, COLS), F32),
        in_specs=vmem(6),
        out_specs=vmem(1)[0],
        scratch_shapes=[
            pltpu.VMEM((SUB, 48, COLS), F32),
            pltpu.VMEM((SUB, HALF, COLS), BF16),
            pltpu.VMEM((SUB, HALF, COLS), BF16),
            pltpu.VMEM((SUB, 2 * TAIL, COLS), BF16),
        ],
        name="finish",
    )(settled, from_left, from_right, wind, lhs, coef)
    return out.reshape(spectra.shape)


def solution(mesh):
    return jax.shard_map(
        body,
        mesh=mesh,
        in_specs=(
            P("gx", None, None, None, "gy"),
            P(),
            P(),
            P(),
            P("gx", None, "gy"),
            P("gx", None, "gy"),
            P("gx", "gy"),
        ),
        out_specs=P("gx", None, None, None, "gy"),
        check_vma=False,
    )
```

```python
import jax
import jax.numpy as jnp
from jax import lax
from jax.experimental import pallas as pl
from jax.experimental.pallas import tpu as pltpu
from jax.sharding import PartitionSpec as P


TYPES = 4
BINS = 33
LEV = 4
BLK = 2
SUB = 2
COLS = 128
ROWS = BLK * TYPES * BINS * LEV
PAIRS = BINS * (BINS + 1) // 2
HALF = 512
TAIL = 64
KDIM = HALF + 2 * TAIL
MROWS = 80
F32 = jnp.float32
BF16 = jnp.bfloat16


def iota(shape, axis):
    return lax.broadcasted_iota(jnp.int32, shape, axis)


def split(x):
    high = x.astype(BF16)
    low = (x - high.astype(F32)).astype(BF16)
    return high, low


def block_row(t, b):
    return (b * TYPES + t) * BINS * LEV


def pair_of_column(col):
    tail = jnp.where(col >= HALF + TAIL, col - TAIL, col)
    first = jnp.where(col < HALF, col & 31, jnp.where(tail < 528, tail - HALF, tail - 528))
    second = jnp.where(
        col < HALF, (first + (col >> 5)) & 31, jnp.where(tail < 528, first + 16, BINS - 1)
    )
    low = jnp.minimum(first, second)
    high = jnp.maximum(first, second)
    pair = low * BINS - ((low * (low - 1)) >> 1) + (high - low)
    return jnp.where(tail > 560, -1, pair)


def edge_kernel(spec, sat, wind, cloudy, edge):
    lane = iota((1, COLS), 1)
    owner = ((lane + 2) & 127) >> 2
    row8 = iota((8, COLS), 0)
    main = [jnp.zeros((8, COLS), F32) for _ in range(4)]
    last = jnp.zeros((8, COLS), F32)
    for b in range(BLK):
        cloud_row = cloudy[b : b + 1, :].astype(F32)
        for l in range(LEV):
            extra = jnp.where(
                row8 == 1,
                sat[b * LEV + l : b * LEV + l + 1, :],
                jnp.where(row8 == 2, wind[b * LEV + l : b * LEV + l + 1, :], cloud_row),
            )
            for t in range(TYPES):
                spot = (t * BLK + b) * LEV + l
                mine = owner == spot
                start = block_row(t, b) + l
                for q in range(4):
                    piece = spec[pl.ds(start + 32 * q, 8, stride=LEV), :]
                    main[q] = jnp.where(mine, pltpu.roll(piece, 4 * spot, 1), main[q])
                piece = jnp.where(row8 == 0, spec[start + 128 : start + 129, :], extra)
                last = jnp.where(mine, pltpu.roll(piece, 4 * spot, 1), last)
    for q in range(4):
        edge[8 * q : 8 * q + 8, :] = main[q]
    edge[32:40, :] = last


def prepare(coll, growth, fall, lhs, coef, raw, parts):
    stacked = jnp.concatenate(
        [
            jnp.concatenate([growth[...], fall[...]], axis=0),
            jnp.zeros((COLS - 2 * TYPES, BINS), F32),
        ],
        axis=0,
    )
    stacked = jnp.concatenate([stacked, jnp.zeros((COLS, COLS - BINS), F32)], axis=1)
    turned = jnp.transpose(stacked)[0:40, :]
    for n in range(2 * TYPES):
        coef[n] = jnp.broadcast_to(turned[:, n : n + 1], (40, COLS))
    raw[...] = jnp.zeros(raw.shape, F32)
    for n in range(KDIM // COLS):
        width = min(COLS, PAIRS - COLS * n)
        for k in range(BINS):
            raw[n, TYPES * k : TYPES * k + TYPES, 0:width] = coll[k, :, COLS * n : COLS * n + width]
    for t in range(TYPES):
        for n in range(KDIM // COLS):
            rows = raw[n, pl.ds(t, 40, stride=TYPES), :]
            both = jnp.concatenate(split(rows), axis=0)
            parts[MROWS * t : MROWS * t + MROWS, COLS * n : COLS * n + COLS] = both
    wanted = pair_of_column(iota((1, KDIM), 1))
    chosen = jnp.where(iota((KDIM, KDIM), 0) == wanted, 1.0, 0.0).astype(BF16)
    lhs[...] = jnp.dot(parts[...], chosen, preferred_element_type=F32).astype(BF16)


def condense(main, top, sat, rate_main, rate_top):
    rising = jnp.maximum(sat, 0.0)
    falling = jnp.maximum(-sat, 0.0)
    transfer = rate_main * main
    up = rising * transfer
    down = falling * transfer
    down_top = falling * (rate_top * top)
    arrive_up = jnp.concatenate([jnp.zeros_like(top), up[:-1]], axis=0)
    arrive_down = jnp.concatenate([down[1:], down_top], axis=0)
    new_main = main - up - down + arrive_up + arrive_down
    new_top = top - down_top + up[-1:]
    return new_main, new_top


def pair_parts(groups, turns):
    for (main, top), turn in zip(groups, turns):
        turn[0:32, :] = main
        turn[32:48, :] = main[0:16]

    def gather(pieces):
        return jnp.concatenate(pieces, axis=1) if len(pieces) > 1 else pieces[0]

    for first in range(0, 16, 4):
        tiles = []
        for (main, _), turn in zip(groups, turns):
            parts = [
                split(main * (main if d == 0 else turn[d : d + 32, :]))
                for d in range(first, first + 4)
            ]
            tiles.append(jnp.concatenate([p[0] for p in parts] + [p[1] for p in parts], axis=0))
        columns = slice(32 * first, 32 * first + 128)
        yield (columns, columns), gather(tiles)
    tails = []
    for main, top in groups:
        square = jnp.where(iota((16, COLS), 0) == 0, top * top, 0.0)
        rest = jnp.concatenate([main[0:16] * main[16:32], main * top, square], axis=0)
        tails.append(jnp.concatenate(split(rest), axis=0))
    yield (slice(HALF, KDIM),), gather(tails)


def collect(lhs, groups, turns):
    total = None
    for columns, part in pair_parts(groups, turns):
        gain = jnp.dot(
            jnp.concatenate([lhs[:, c] for c in columns], axis=1), part, preferred_element_type=F32
        )
        total = gain if total is None else total + gain
    return total


def shares():
    x, y = lax.axis_index("gx"), lax.axis_index("gy")
    size = lax.axis_size("gy")
    odd = (y & 1) == 1
    origin = (x == 0) & (y == 0)
    total = BLK * TYPES
    first = jnp.where(odd & (y < size - 1), jnp.where(y < size // 2, 3, 1), 0)
    first = jnp.where((y == 0) & jnp.logical_not(origin), total, first)
    second = jnp.where(origin | (y == size - 1), first, total)
    return (0, first), (first, second), (second, total)


def main_kernel(which, spec, sat, cloudy, coll, growth, fall, edge, *rest):
    settled, lhs, coef = rest[-7:-4] if which < 2 else rest[-6:-3]
    turn, raw, parts = rest[-3:]
    if which < 2:
        rest[-4][...] = edge[...]
    begin, end = shares()[which]

    @pl.when((begin == 0) & (end > 0))
    def _():
        prepare(coll, growth, fall, lhs, coef, raw, parts)

    def one(n, carry):
        t = n >> 1
        b = n & 1
        start = block_row(t, b)
        left = lhs[pl.ds(pl.multiple_of(t * MROWS, 16), MROWS), :]
        rate = coef[t]
        speed = coef[TYPES + t]
        wet = cloudy[pl.ds(b, 1), :] > 0
        before = []
        state = []
        for l in range(LEV):
            main = spec[pl.ds(start + l, 32, stride=LEV), :]
            top = spec[pl.ds(start + 128 + l, 1), :]
            before.append((main, top))
            row = sat[pl.ds(b * LEV + l, 1), :]
            state.append(condense(main, top, row, rate[0:32], rate[32:33]))
        for step in range(SUB):
            for half in range(2):
                levels = range(2 * half, 2 * half + 2)
                gain = collect(
                    left,
                    [state[l] for l in levels],
                    [turn.at[LEV * step + l] for l in levels],
                )
                for k in range(2):
                    l = 2 * half + k
                    mine = gain[:, COLS * k : COLS * k + COLS]
                    main, top = state[l]
                    state[l] = (
                        main + (mine[0:32] + mine[40:72]),
                        top + (mine[32:33] + mine[72:73]),
                    )
        above = None
        for l in reversed(range(LEV)):
            main = jnp.where(wet, state[l][0], before[l][0])
            top = jnp.where(wet, state[l][1], before[l][1])
            over = (jnp.zeros_like(main), jnp.zeros_like(top)) if above is None else above
            settled[n, l, 0:32, :] = main + speed[0:32] * (over[0] - main)
            settled[n, l, 32:33, :] = top + speed[32:33] * (over[1] - top)
            above = (main, top)
        return carry

    lax.fori_loop(begin, end, one, 0)


def finish_kernel(settled, even0, odd0, even1, odd1, edge, wind, lhs, coef, out, turn, result, sems):
    lane = iota((1, COLS), 1)
    owner = ((lane + 2) & 127) >> 2
    kind = owner >> 3
    place = lane & 3
    even = even0[...] + even1[...]
    odd = odd0[...] + odd1[...]
    mine_odd = (lax.axis_index("gy") & 1) * 2
    halo = jnp.where((lane & 2) == mine_odd, even, odd)

    def by_type(pieces):
        value = pieces[0]
        for t in range(1, TYPES):
            value = jnp.where(kind == t, pieces[t], value)
        return value

    rate = by_type([coef[t] for t in range(TYPES)])
    speed = by_type([coef[TYPES + t] for t in range(TYPES)])
    main = halo[0:32]
    top = halo[32:33]
    wet = halo[35:36] > 0
    state = condense(main, top, halo[33:34], rate[0:32], rate[32:33])
    for step in range(SUB):
        gain = collect(lhs[...], [state], [turn.at[step]])
        share = by_type([gain[MROWS * t : MROWS * t + MROWS] for t in range(TYPES)])
        state = (
            state[0] + (share[0:32] + share[40:72]),
            state[1] + (share[32:33] + share[72:73]),
        )
    highest = (owner & 3) == LEV - 1

    def settle(value, speed):
        above = jnp.where(highest, 0.0, pltpu.roll(value, COLS - 4, 1))
        return value + speed * (above - value)

    ghost = jnp.concatenate(
        [
            settle(jnp.where(wet, state[0], main), speed[0:32]),
            settle(jnp.broadcast_to(jnp.where(wet, state[1], top), (8, COLS)), speed[32:40]),
        ],
        axis=0,
    )

    def weights(left, right):
        left_abs = jnp.abs(left)
        right_abs = jnp.abs(right)
        return (
            left_abs - left,
            (right - right_abs) + (7.0 * left - 3.0 * left_abs),
            1.0 - (7.0 * right - 3.0 * right_abs) + (7.0 * left + 3.0 * left_abs),
            -(7.0 * right + 3.0 * right_abs) - (left + left_abs),
            right + right_abs,
        )

    scale = 0.5 / 12.0
    far = jnp.broadcast_to(halo[34:35], (8, COLS))
    near = jnp.broadcast_to(edge[34:35], (8, COLS))
    lower = jnp.where(place == 0, pltpu.roll(far, 1, 1), pltpu.roll(near, 1, 1))
    upper = jnp.where(place == 3, pltpu.roll(far, COLS - 1, 1), pltpu.roll(near, COLS - 1, 1))
    w = weights((near + lower) * scale, (near + upper) * scale)
    weight_2 = jnp.where(place < 2, w[0], w[4])[0:1]
    weight_1 = jnp.where(place == 0, w[1], jnp.where(place == 3, w[3], 0.0))[0:1]
    by_2 = jnp.where(place < 2, pltpu.roll(ghost, 2, 1), pltpu.roll(ghost, COLS - 2, 1))
    by_1 = jnp.where(place == 0, pltpu.roll(ghost, 1, 1), pltpu.roll(ghost, COLS - 1, 1))
    extra = weight_2 * by_2 + weight_1 * by_1

    row = iota((2 * COLS, COLS), 0) & (COLS - 1)
    col = iota((2 * COLS, COLS), 1)
    shift = jnp.concatenate(
        [jnp.where(row == col + by, 1.0, 0.0).astype(BF16) for by in (-2, -1, 1, 2)], axis=1
    )
    outer = (lane < 2) | (lane >= COLS - 2)
    for b in range(BLK):
        for l in range(LEV):
            at = b * LEV + l
            own = jnp.broadcast_to(wind[at : at + 1, :], (8, COLS))
            beyond = pltpu.roll(far, (COLS - 4 * at) % COLS, 1)
            lower = pltpu.roll(jnp.where(lane == COLS - 1, beyond, own), 1, 1)
            upper = pltpu.roll(jnp.where(lane == 0, beyond, own), COLS - 1, 1)
            w = weights((own + lower) * scale, (own + upper) * scale)
            x = jnp.concatenate([settled[t * BLK + b, l] for t in range(TYPES)], axis=0)
            moved = jnp.dot(
                jnp.concatenate(split(x), axis=1), shift, preferred_element_type=F32
            )
            for t in range(TYPES):
                rows = slice(40 * t, 40 * t + 40)
                spot = (t * BLK + b) * LEV + l
                added = jnp.where(outer, pltpu.roll(extra, (COLS - 4 * spot) % COLS, 1), 0.0)
                y = w[2][0:1] * x[rows] + added
                for n, k in enumerate((0, 1, 3, 4)):
                    y = y + w[k][0:1] * moved[rows, COLS * n : COLS * n + COLS]
                start = block_row(t, b) + l
                for q in range(4):
                    result[pl.ds(start + 32 * q, 8, stride=LEV), :] = y[8 * q : 8 * q + 8]
                result[start + 128 : start + 129, :] = y[32:33]
        rows = pl.ds(b * (ROWS // BLK), ROWS // BLK)
        pltpu.make_async_copy(result.at[rows], out.at[rows], sems.at[b]).start()
    for b in range(BLK):
        rows = pl.ds(b * (ROWS // BLK), ROWS // BLK)
        pltpu.make_async_copy(result.at[rows], out.at[rows], sems.at[b]).wait()


def vmem(count):
    return [pl.BlockSpec(memory_space=pltpu.VMEM)] * count


def resident(*arrays):
    return [pltpu.with_memory_space_constraint(x, pltpu.VMEM) for x in arrays]


def swaps(pairs):
    return [(a, b) for a, b in pairs] + [(b, a) for a, b in pairs]


def body(spectra, collection, growth_rate, fall_speed, supersaturation, courant, cloudy):
    spec = spectra.reshape(ROWS, COLS)
    sat = supersaturation.reshape(BLK * LEV, COLS)
    wind = courant.reshape(BLK * LEV, COLS)
    coll = jnp.transpose(collection, (1, 0, 2))
    wide, long = lax.axis_size("gx"), lax.axis_size("gy")

    def device(x, y):
        return x * long + y % long

    early, middle, late, origin = [], [], [], []
    for x in range(wide):
        for y in range(0, long, 2):
            pair = (device(x, y), device(x, y + 1))
            (origin if x == 0 and y == 0 else early).append(pair)
            pair = (device(x, y + 1), device(x, y + 2))
            (late if y + 2 == long else middle).append(pair)

    def exchange(edge, pairs):
        return lax.ppermute(edge, ("gx", "gy"), swaps(pairs))

    edge = pl.pallas_call(
        edge_kernel,
        out_shape=pltpu.VMEM((40, COLS), F32),
        in_specs=vmem(4),
        out_specs=vmem(1)[0],
        name="edges",
    )(*resident(spec, sat, wind, cloudy))

    def blocks(which, edge, held):
        shapes = (
            pltpu.VMEM((BLK * TYPES, LEV, 40, COLS), F32),
            pltpu.VMEM((TYPES * MROWS, KDIM), BF16),
            pltpu.VMEM((2 * TYPES, 40, COLS), F32),
        )
        if which < 2:
            shapes += (pltpu.VMEM((40, COLS), F32),)
        return pl.pallas_call(
            lambda *refs: main_kernel(which, *refs),
            out_shape=shapes,
            in_specs=vmem(7 + len(held)),
            out_specs=tuple(vmem(len(shapes))),
            input_output_aliases={7 + n: n for n in range(len(held))},
            scratch_shapes=[
                pltpu.VMEM((SUB * LEV, 48, COLS), F32),
                pltpu.VMEM((KDIM // COLS, TYPES * 40, COLS), F32),
                pltpu.VMEM((TYPES * MROWS, KDIM), BF16),
            ],
        )(*resident(spec, sat, cloudy, coll, growth_rate, fall_speed, edge, *held))

    even0 = exchange(edge, early)
    *held, edge0 = blocks(0, edge, ())
    odd0 = exchange(edge0, middle)
    *held, edge1 = blocks(1, edge0, held)
    even1 = exchange(edge1, origin)
    odd1 = exchange(edge1, late)
    settled, lhs, coef = blocks(2, edge1, held)
    out = pl.pallas_call(
        finish_kernel,
        out_shape=jax.ShapeDtypeStruct((ROWS, COLS), F32),
        in_specs=vmem(9),
        out_specs=pl.BlockSpec(memory_space=pl.ANY),
        scratch_shapes=[
            pltpu.VMEM((SUB, 48, COLS), F32),
            pltpu.VMEM((ROWS, COLS), F32),
            pltpu.SemaphoreType.DMA((BLK,)),
        ],
        name="finish",
    )(*resident(settled, even0, odd0, even1, odd1, edge, wind, lhs, coef))
    return out.reshape(spectra.shape)


def solution(mesh):
    return jax.shard_map(
        body,
        mesh=mesh,
        in_specs=(
            P("gx", None, None, None, "gy"),
            P(),
            P(),
            P(),
            P("gx", None, "gy"),
            P("gx", None, "gy"),
            P("gx", "gy"),
        ),
        out_specs=P("gx", None, None, None, "gy"),
        check_vma=False,
    )
```

```python
import jax
import jax.numpy as jnp
from jax import lax
from jax.experimental import pallas as pl
from jax.experimental.pallas import tpu as pltpu
from jax.sharding import PartitionSpec as P


TYPES = 4
BINS = 33
LEV = 4
BLK = 2
SUB = 2
COLS = 128
ROWS = BLK * TYPES * BINS * LEV
PAIRS = BINS * (BINS + 1) // 2
HALF = 512
TAIL = 64
KDIM = HALF + 2 * TAIL
MROWS = 80
F32 = jnp.float32
BF16 = jnp.bfloat16


def iota(shape, axis):
    return lax.broadcasted_iota(jnp.int32, shape, axis)


def split(x):
    high = x.astype(BF16)
    low = (x - high.astype(F32)).astype(BF16)
    return high, low


def block_row(t, b):
    return (b * TYPES + t) * BINS * LEV


def pair_of_column(col):
    tail = jnp.where(col >= HALF + TAIL, col - TAIL, col)
    first = jnp.where(col < HALF, col & 31, jnp.where(tail < 528, tail - HALF, tail - 528))
    second = jnp.where(
        col < HALF, (first + (col >> 5)) & 31, jnp.where(tail < 528, first + 16, BINS - 1)
    )
    low = jnp.minimum(first, second)
    high = jnp.maximum(first, second)
    pair = low * BINS - ((low * (low - 1)) >> 1) + (high - low)
    return jnp.where(tail > 560, -1, pair)


def edge_kernel(*refs):
    sources, edge, kept, sems = refs[:7], refs[7], refs[8:15], refs[15]
    copies = [
        pltpu.make_async_copy(src, dst, sems.at[n])
        for n, (src, dst) in enumerate(zip(sources, kept))
    ]
    for copy in copies:
        copy.start()
    spec, sat, wind, cloudy = kept[:4]
    for copy in copies[:4]:
        copy.wait()
    lane = iota((1, COLS), 1)
    owner = ((lane + 2) & 127) >> 2
    row8 = iota((8, COLS), 0)
    main = [jnp.zeros((8, COLS), F32) for _ in range(4)]
    last = jnp.zeros((8, COLS), F32)
    for b in range(BLK):
        cloud_row = cloudy[b : b + 1, :].astype(F32)
        for l in range(LEV):
            extra = jnp.where(
                row8 == 1,
                sat[b * LEV + l : b * LEV + l + 1, :],
                jnp.where(row8 == 2, wind[b * LEV + l : b * LEV + l + 1, :], cloud_row),
            )
            for t in range(TYPES):
                spot = (t * BLK + b) * LEV + l
                mine = owner == spot
                start = block_row(t, b) + l
                for q in range(4):
                    piece = spec[pl.ds(start + 32 * q, 8, stride=LEV), :]
                    main[q] = jnp.where(mine, pltpu.roll(piece, 4 * spot, 1), main[q])
                piece = jnp.where(row8 == 0, spec[start + 128 : start + 129, :], extra)
                last = jnp.where(mine, pltpu.roll(piece, 4 * spot, 1), last)
    for q in range(4):
        edge[8 * q : 8 * q + 8, :] = main[q]
    edge[32:40, :] = last
    for copy in copies[4:]:
        copy.wait()


def prepare(coll, growth, fall, lhs, coef, raw, parts):
    stacked = jnp.concatenate(
        [
            jnp.concatenate([growth[...], fall[...]], axis=0),
            jnp.zeros((COLS - 2 * TYPES, BINS), F32),
        ],
        axis=0,
    )
    stacked = jnp.concatenate([stacked, jnp.zeros((COLS, COLS - BINS), F32)], axis=1)
    turned = jnp.transpose(stacked)[0:40, :]
    for n in range(2 * TYPES):
        coef[n] = jnp.broadcast_to(turned[:, n : n + 1], (40, COLS))
    raw[...] = jnp.zeros(raw.shape, F32)
    for n in range(KDIM // COLS):
        width = min(COLS, PAIRS - COLS * n)
        for k in range(BINS):
            raw[n, TYPES * k : TYPES * k + TYPES, 0:width] = coll[k, :, COLS * n : COLS * n + width]
    for t in range(TYPES):
        for n in range(KDIM // COLS):
            rows = raw[n, pl.ds(t, 40, stride=TYPES), :]
            both = jnp.concatenate(split(rows), axis=0)
            parts[MROWS * t : MROWS * t + MROWS, COLS * n : COLS * n + COLS] = both
    wanted = pair_of_column(iota((1, KDIM), 1))
    chosen = jnp.where(iota((KDIM, KDIM), 0) == wanted, 1.0, 0.0).astype(BF16)
    lhs[...] = jnp.dot(parts[...], chosen, preferred_element_type=F32).astype(BF16)


def condense(main, top, sat, rate_main, rate_top):
    rising = jnp.maximum(sat, 0.0)
    falling = jnp.maximum(-sat, 0.0)
    transfer = rate_main * main
    up = rising * transfer
    down = falling * transfer
    down_top = falling * (rate_top * top)
    arrive_up = jnp.concatenate([jnp.zeros_like(top), up[:-1]], axis=0)
    arrive_down = jnp.concatenate([down[1:], down_top], axis=0)
    new_main = main - up - down + arrive_up + arrive_down
    new_top = top - down_top + up[-1:]
    return new_main, new_top


def pair_parts(groups, turns):
    for (main, top), turn in zip(groups, turns):
        turn[0:32, :] = main
        turn[32:48, :] = main[0:16]

    def gather(pieces):
        return jnp.concatenate(pieces, axis=1) if len(pieces) > 1 else pieces[0]

    for first in range(0, 16, 4):
        tiles = []
        for (main, _), turn in zip(groups, turns):
            parts = [
                split(main * (main if d == 0 else turn[d : d + 32, :]))
                for d in range(first, first + 4)
            ]
            tiles.append(jnp.concatenate([p[0] for p in parts] + [p[1] for p in parts], axis=0))
        columns = slice(32 * first, 32 * first + 128)
        yield (columns, columns), gather(tiles)
    tails = []
    for main, top in groups:
        square = jnp.where(iota((16, COLS), 0) == 0, top * top, 0.0)
        rest = jnp.concatenate([main[0:16] * main[16:32], main * top, square], axis=0)
        tails.append(jnp.concatenate(split(rest), axis=0))
    yield (slice(HALF, KDIM),), gather(tails)


def collect(lhs, groups, turns):
    total = None
    for columns, part in pair_parts(groups, turns):
        gain = jnp.dot(
            jnp.concatenate([lhs[:, c] for c in columns], axis=1), part, preferred_element_type=F32
        )
        total = gain if total is None else total + gain
    return total


def shares():
    x, y = lax.axis_index("gx"), lax.axis_index("gy")
    z = y >> 1
    first = jnp.int32(0)
    for n, count in enumerate((8, 7, 5, 3, 1)):
        first = jnp.where(z == n, count, first)
    first = jnp.where((x == 0) & (y == 0), 0, first)
    return (0, first), (first, BLK * TYPES)


def main_kernel(which, spec, sat, cloudy, coll, growth, fall, edge, *rest):
    settled, lhs, coef = rest[-7:-4] if which == 0 else rest[-6:-3]
    turn, raw, parts = rest[-3:]
    if which == 0:
        rest[-4][...] = edge[...]
    begin, end = shares()[which]

    @pl.when((begin == 0) & (end > 0))
    def _():
        prepare(coll, growth, fall, lhs, coef, raw, parts)

    def one(n, carry):
        t = n >> 1
        b = n & 1
        start = block_row(t, b)
        left = lhs[pl.ds(pl.multiple_of(t * MROWS, 16), MROWS), :]
        rate = coef[t]
        speed = coef[TYPES + t]
        wet = cloudy[pl.ds(b, 1), :] > 0
        before = []
        state = []
        for l in range(LEV):
            main = spec[pl.ds(start + l, 32, stride=LEV), :]
            top = spec[pl.ds(start + 128 + l, 1), :]
            before.append((main, top))
            row = sat[pl.ds(b * LEV + l, 1), :]
            state.append(condense(main, top, row, rate[0:32], rate[32:33]))
        for step in range(SUB):
            for half in range(2):
                levels = range(2 * half, 2 * half + 2)
                gain = collect(
                    left,
                    [state[l] for l in levels],
                    [turn.at[LEV * step + l] for l in levels],
                )
                for k in range(2):
                    l = 2 * half + k
                    mine = gain[:, COLS * k : COLS * k + COLS]
                    main, top = state[l]
                    state[l] = (
                        main + (mine[0:32] + mine[40:72]),
                        top + (mine[32:33] + mine[72:73]),
                    )
        above = None
        for l in reversed(range(LEV)):
            main = jnp.where(wet, state[l][0], before[l][0])
            top = jnp.where(wet, state[l][1], before[l][1])
            over = (jnp.zeros_like(main), jnp.zeros_like(top)) if above is None else above
            settled[n, l, 0:32, :] = main + speed[0:32] * (over[0] - main)
            settled[n, l, 32:33, :] = top + speed[32:33] * (over[1] - top)
            above = (main, top)
        return carry

    lax.fori_loop(begin, end, one, 0)


def finish_kernel(settled, from_left, from_right, edge, wind, lhs, coef, out, turn, result, sems):
    lane = iota((1, COLS), 1)
    owner = ((lane + 2) & 127) >> 2
    kind = owner >> 3
    place = lane & 3
    halo = jnp.where(place < 2, from_right[...], from_left[...])

    def by_type(pieces):
        value = pieces[0]
        for t in range(1, TYPES):
            value = jnp.where(kind == t, pieces[t], value)
        return value

    rate = by_type([coef[t] for t in range(TYPES)])
    speed = by_type([coef[TYPES + t] for t in range(TYPES)])
    main = halo[0:32]
    top = halo[32:33]
    wet = halo[35:36] > 0
    state = condense(main, top, halo[33:34], rate[0:32], rate[32:33])
    for step in range(SUB):
        gain = collect(lhs[...], [state], [turn.at[step]])
        share = by_type([gain[MROWS * t : MROWS * t + MROWS] for t in range(TYPES)])
        state = (
            state[0] + (share[0:32] + share[40:72]),
            state[1] + (share[32:33] + share[72:73]),
        )
    highest = (owner & 3) == LEV - 1

    def settle(value, speed):
        above = jnp.where(highest, 0.0, pltpu.roll(value, COLS - 4, 1))
        return value + speed * (above - value)

    ghost = jnp.concatenate(
        [
            settle(jnp.where(wet, state[0], main), speed[0:32]),
            settle(jnp.broadcast_to(jnp.where(wet, state[1], top), (8, COLS)), speed[32:40]),
        ],
        axis=0,
    )

    def weights(left, right):
        left_abs = jnp.abs(left)
        right_abs = jnp.abs(right)
        return (
            left_abs - left,
            (right - right_abs) + (7.0 * left - 3.0 * left_abs),
            1.0 - (7.0 * right - 3.0 * right_abs) + (7.0 * left + 3.0 * left_abs),
            -(7.0 * right + 3.0 * right_abs) - (left + left_abs),
            right + right_abs,
        )

    scale = 0.5 / 12.0
    far = jnp.broadcast_to(halo[34:35], (8, COLS))
    near = jnp.broadcast_to(edge[34:35], (8, COLS))
    lower = jnp.where(place == 0, pltpu.roll(far, 1, 1), pltpu.roll(near, 1, 1))
    upper = jnp.where(place == 3, pltpu.roll(far, COLS - 1, 1), pltpu.roll(near, COLS - 1, 1))
    w = weights((near + lower) * scale, (near + upper) * scale)
    weight_2 = jnp.where(place < 2, w[0], w[4])[0:1]
    weight_1 = jnp.where(place == 0, w[1], jnp.where(place == 3, w[3], 0.0))[0:1]
    by_2 = jnp.where(place < 2, pltpu.roll(ghost, 2, 1), pltpu.roll(ghost, COLS - 2, 1))
    by_1 = jnp.where(place == 0, pltpu.roll(ghost, 1, 1), pltpu.roll(ghost, COLS - 1, 1))
    extra = weight_2 * by_2 + weight_1 * by_1

    row = iota((2 * COLS, COLS), 0) & (COLS - 1)
    col = iota((2 * COLS, COLS), 1)
    shift = jnp.concatenate(
        [jnp.where(row == col + by, 1.0, 0.0).astype(BF16) for by in (-2, -1, 1, 2)], axis=1
    )
    outer = (lane < 2) | (lane >= COLS - 2)
    for b in range(BLK):
        for l in range(LEV):
            at = b * LEV + l
            own = jnp.broadcast_to(wind[at : at + 1, :], (8, COLS))
            beyond = pltpu.roll(far, (COLS - 4 * at) % COLS, 1)
            lower = pltpu.roll(jnp.where(lane == COLS - 1, beyond, own), 1, 1)
            upper = pltpu.roll(jnp.where(lane == 0, beyond, own), COLS - 1, 1)
            w = weights((own + lower) * scale, (own + upper) * scale)
            x = jnp.concatenate([settled[t * BLK + b, l] for t in range(TYPES)], axis=0)
            moved = jnp.dot(
                jnp.concatenate(split(x), axis=1), shift, preferred_element_type=F32
            )
            for t in range(TYPES):
                rows = slice(40 * t, 40 * t + 40)
                spot = (t * BLK + b) * LEV + l
                added = jnp.where(outer, pltpu.roll(extra, (COLS - 4 * spot) % COLS, 1), 0.0)
                y = w[2][0:1] * x[rows] + added
                for n, k in enumerate((0, 1, 3, 4)):
                    y = y + w[k][0:1] * moved[rows, COLS * n : COLS * n + COLS]
                start = block_row(t, b) + l
                for q in range(4):
                    result[pl.ds(start + 32 * q, 8, stride=LEV), :] = y[8 * q : 8 * q + 8]
                result[start + 128 : start + 129, :] = y[32:33]
        rows = pl.ds(b * (ROWS // BLK), ROWS // BLK)
        pltpu.make_async_copy(result.at[rows], out.at[rows], sems.at[b]).start()
    for b in range(BLK):
        rows = pl.ds(b * (ROWS // BLK), ROWS // BLK)
        pltpu.make_async_copy(result.at[rows], out.at[rows], sems.at[b]).wait()


def vmem(count):
    return [pl.BlockSpec(memory_space=pltpu.VMEM)] * count


def resident(*arrays):
    return [pltpu.with_memory_space_constraint(x, pltpu.VMEM) for x in arrays]


def body(spectra, collection, growth_rate, fall_speed, supersaturation, courant, cloudy):
    sources = (
        spectra.reshape(ROWS, COLS),
        supersaturation.reshape(BLK * LEV, COLS),
        courant.reshape(BLK * LEV, COLS),
        cloudy,
        jnp.transpose(collection, (1, 0, 2)),
        growth_rate,
        fall_speed,
    )
    edge, spec, sat, wind, wet, coll, growth, fall = pl.pallas_call(
        edge_kernel,
        out_shape=(pltpu.VMEM((40, COLS), F32), *(pltpu.VMEM(x.shape, x.dtype) for x in sources)),
        in_specs=[pl.BlockSpec(memory_space=pl.ANY)] * len(sources),
        out_specs=tuple(vmem(1 + len(sources))),
        scratch_shapes=[pltpu.SemaphoreType.DMA((len(sources),))],
        name="edges",
    )(*sources)

    def blocks(which, edge, held):
        shapes = (
            pltpu.VMEM((BLK * TYPES, LEV, 40, COLS), F32),
            pltpu.VMEM((TYPES * MROWS, KDIM), BF16),
            pltpu.VMEM((2 * TYPES, 40, COLS), F32),
        )
        if which == 0:
            shapes += (pltpu.VMEM((40, COLS), F32),)
        return pl.pallas_call(
            lambda *refs: main_kernel(which, *refs),
            out_shape=shapes,
            in_specs=vmem(7 + len(held)),
            out_specs=tuple(vmem(len(shapes))),
            input_output_aliases={7 + n: n for n in range(len(held))},
            scratch_shapes=[
                pltpu.VMEM((SUB * LEV, 48, COLS), F32),
                pltpu.VMEM((KDIM // COLS, TYPES * 40, COLS), F32),
                pltpu.VMEM((TYPES * MROWS, KDIM), BF16),
            ],
        )(*resident(spec, sat, wet, coll, growth, fall, edge, *held))

    count = lax.axis_size("gy")
    up = [(i, (i + 1) % count) for i in range(count)]
    down = [(j, i) for i, j in up]
    *held, packed = blocks(0, edge, ())
    from_left = lax.ppermute(packed, "gy", up)
    from_right = lax.ppermute(packed, "gy", down)
    settled, lhs, coef = blocks(1, packed, held)
    out = pl.pallas_call(
        finish_kernel,
        out_shape=jax.ShapeDtypeStruct((ROWS, COLS), F32),
        in_specs=vmem(7),
        out_specs=pl.BlockSpec(memory_space=pl.ANY),
        scratch_shapes=[
            pltpu.VMEM((SUB, 48, COLS), F32),
            pltpu.VMEM((ROWS, COLS), F32),
            pltpu.SemaphoreType.DMA((BLK,)),
        ],
        name="finish",
    )(*resident(settled, from_left, from_right, edge, wind, lhs, coef))
    return out.reshape(spectra.shape)


def solution(mesh):
    return jax.shard_map(
        body,
        mesh=mesh,
        in_specs=(
            P("gx", None, None, None, "gy"),
            P(),
            P(),
            P(),
            P("gx", None, "gy"),
            P("gx", None, "gy"),
            P("gx", "gy"),
        ),
        out_specs=P("gx", None, None, None, "gy"),
        check_vma=False,
    )
```

```python
import jax
import jax.numpy as jnp
from jax import lax
from jax.experimental import pallas as pl
from jax.experimental.pallas import tpu as pltpu
from jax.sharding import PartitionSpec as P


TYPES = 4
BINS = 33
LEV = 4
BLK = 2
SUB = 2
COLS = 128
ROWS = BLK * TYPES * BINS * LEV
PAIRS = BINS * (BINS + 1) // 2
HALF = 512
TAIL = 64
KDIM = HALF + 2 * TAIL
MROWS = 80
SCALE = 0.5 / 12.0
F32 = jnp.float32
BF16 = jnp.bfloat16


def iota(shape, axis):
    return lax.broadcasted_iota(jnp.int32, shape, axis)


def split(x):
    high = x.astype(BF16)
    low = (x - high.astype(F32)).astype(BF16)
    return high, low


def block_row(t, b):
    return (b * TYPES + t) * BINS * LEV


def pair_of_column(col):
    tail = jnp.where(col >= HALF + TAIL, col - TAIL, col)
    first = jnp.where(col < HALF, col & 31, jnp.where(tail < 528, tail - HALF, tail - 528))
    second = jnp.where(
        col < HALF, (first + (col >> 5)) & 31, jnp.where(tail < 528, first + 16, BINS - 1)
    )
    low = jnp.minimum(first, second)
    high = jnp.maximum(first, second)
    pair = low * BINS - ((low * (low - 1)) >> 1) + (high - low)
    return jnp.where(tail > 560, -1, pair)


def edge_kernel(*refs):
    sources, edge, chosen, kept, sems = refs[:7], refs[7], refs[8], refs[9:16], refs[16]
    halves = [pl.ds(b * (ROWS // BLK), ROWS // BLK) for b in range(BLK)]
    pairs = [(sources[0].at[rows], kept[0].at[rows]) for rows in halves]
    pairs += list(zip(sources[1:], kept[1:]))
    copies = [pltpu.make_async_copy(*pair, sems.at[n]) for n, pair in enumerate(pairs)]
    for n in (2, 3, 4, 0, 1, 5, 6, 7):
        copies[n].start()
    wanted = pair_of_column(iota((1, KDIM), 1))
    for first in range(0, KDIM, COLS):
        rows = iota((COLS, KDIM), 0) + first
        chosen[first : first + COLS, :] = jnp.where(rows == wanted, 1.0, 0.0).astype(BF16)
    spec, sat, wind, cloudy = kept[:4]
    for copy in copies[2:5]:
        copy.wait()
    lane = iota((1, COLS), 1)
    owner = ((lane + 2) & 127) >> 2
    row8 = iota((8, COLS), 0)
    main = [jnp.zeros((8, COLS), F32) for _ in range(4)]
    last = jnp.zeros((8, COLS), F32)
    for b in range(BLK):
        copies[b].wait()
        cloud_row = cloudy[b : b + 1, :].astype(F32)
        for l in range(LEV):
            extra = jnp.where(
                row8 == 1,
                sat[b * LEV + l : b * LEV + l + 1, :],
                jnp.where(row8 == 2, wind[b * LEV + l : b * LEV + l + 1, :], cloud_row),
            )
            for t in range(TYPES):
                spot = (t * BLK + b) * LEV + l
                mine = owner == spot
                start = block_row(t, b) + l
                for q in range(4):
                    piece = spec[pl.ds(start + 32 * q, 8, stride=LEV), :]
                    main[q] = jnp.where(mine, pltpu.roll(piece, 4 * spot, 1), main[q])
                piece = jnp.where(row8 == 0, spec[start + 128 : start + 129, :], extra)
                last = jnp.where(mine, pltpu.roll(piece, 4 * spot, 1), last)
    for q in range(4):
        edge[8 * q : 8 * q + 8, :] = main[q]
    edge[32:40, :] = last
    for copy in copies[5:]:
        copy.wait()


def weights(left, right):
    left_abs = jnp.abs(left)
    right_abs = jnp.abs(right)
    return (
        left_abs - left,
        (right - right_abs) + (7.0 * left - 3.0 * left_abs),
        1.0 - (7.0 * right - 3.0 * right_abs) + (7.0 * left + 3.0 * left_abs),
        -(7.0 * right + 3.0 * right_abs) - (left + left_abs),
        right + right_abs,
    )


def prepare(coll, growth, fall, wind, chosen, lhs, coef, stencil, raw, parts):
    stacked = jnp.concatenate(
        [
            jnp.concatenate([growth[...], fall[...]], axis=0),
            jnp.zeros((COLS - 2 * TYPES, BINS), F32),
        ],
        axis=0,
    )
    stacked = jnp.concatenate([stacked, jnp.zeros((COLS, COLS - BINS), F32)], axis=1)
    turned = jnp.transpose(stacked)[0:40, :]
    for n in range(2 * TYPES):
        coef[n] = jnp.broadcast_to(turned[:, n : n + 1], (40, COLS))
    lane = iota((1, COLS), 1)
    own = wind[...]
    left = jnp.where(lane == 0, 0.0, (own + pltpu.roll(own, 1, 1)) * SCALE)
    right = jnp.where(lane == COLS - 1, 0.0, (own + pltpu.roll(own, COLS - 1, 1)) * SCALE)
    for by, value in zip(range(-2, 3), weights(left, right)):
        inside = (lane + by >= 0) & (lane + by < COLS)
        stencil[by + 2] = jnp.where(inside, value, 0.0)
    raw[...] = jnp.zeros(raw.shape, F32)
    for n in range(KDIM // COLS):
        width = min(COLS, PAIRS - COLS * n)
        for k in range(BINS):
            raw[n, TYPES * k : TYPES * k + TYPES, 0:width] = coll[k, :, COLS * n : COLS * n + width]
    for t in range(TYPES):
        for n in range(KDIM // COLS):
            rows = raw[n, pl.ds(t, 40, stride=TYPES), :]
            both = jnp.concatenate(split(rows), axis=0)
            parts[MROWS * t : MROWS * t + MROWS, COLS * n : COLS * n + COLS] = both
    lhs[...] = jnp.dot(parts[...], chosen[...], preferred_element_type=F32).astype(BF16)


def condense(main, top, sat, rate_main, rate_top):
    rising = jnp.maximum(sat, 0.0)
    falling = jnp.maximum(-sat, 0.0)
    transfer = rate_main * main
    up = rising * transfer
    down = falling * transfer
    down_top = falling * (rate_top * top)
    arrive_up = jnp.concatenate([jnp.zeros_like(top), up[:-1]], axis=0)
    arrive_down = jnp.concatenate([down[1:], down_top], axis=0)
    new_main = main - up - down + arrive_up + arrive_down
    new_top = top - down_top + up[-1:]
    return new_main, new_top


def pair_parts(groups, turns):
    for (main, top), turn in zip(groups, turns):
        turn[0:32, :] = main
        turn[32:48, :] = main[0:16]

    def gather(pieces):
        return jnp.concatenate(pieces, axis=1) if len(pieces) > 1 else pieces[0]

    for first in range(0, 16, 4):
        tiles = []
        for (main, _), turn in zip(groups, turns):
            parts = [
                split(main * (main if d == 0 else turn[d : d + 32, :]))
                for d in range(first, first + 4)
            ]
            tiles.append(jnp.concatenate([p[0] for p in parts] + [p[1] for p in parts], axis=0))
        columns = slice(32 * first, 32 * first + 128)
        yield (columns, columns), gather(tiles)
    tails = []
    for main, top in groups:
        square = jnp.where(iota((16, COLS), 0) == 0, top * top, 0.0)
        rest = jnp.concatenate([main[0:16] * main[16:32], main * top, square], axis=0)
        tails.append(jnp.concatenate(split(rest), axis=0))
    yield (slice(HALF, KDIM),), gather(tails)


def collect(lhs, groups, turns):
    total = None
    for columns, part in pair_parts(groups, turns):
        gain = jnp.dot(
            jnp.concatenate([lhs[:, c] for c in columns], axis=1), part, preferred_element_type=F32
        )
        total = gain if total is None else total + gain
    return total


def collect_apart(lhs, main, top, turn):
    turn[0:32, :] = main
    turn[32:48, :] = main[0:16]
    total = None
    for first in range(0, 16, 8):
        value = jnp.concatenate(
            [main * (main if d == 0 else turn[d : d + 32, :]) for d in range(first, first + 8)],
            axis=0,
        )
        part = jnp.concatenate(split(value), axis=1)
        gain = jnp.dot(lhs[:, 32 * first : 32 * first + 256], part, preferred_element_type=F32)
        total = gain if total is None else total + gain
    square = jnp.where(iota((16, COLS), 0) == 0, top * top, 0.0)
    rest = jnp.concatenate([main[0:16] * main[16:32], main * top, square], axis=0)
    part = jnp.concatenate(split(rest), axis=1)
    total = total + jnp.dot(lhs[:, HALF : HALF + TAIL], part, preferred_element_type=F32)
    return total[:, 0:COLS] + total[:, COLS : 2 * COLS]


def shares():
    x, y = lax.axis_index("gx"), lax.axis_index("gy")
    z = y >> 1
    first = jnp.int32(0)
    for n, count in enumerate((8, 7, 5, 3, 1)):
        first = jnp.where(z == n, count, first)
    first = jnp.where((x == 0) & (y == 0), 0, first)
    return (0, first), (first, BLK * TYPES)


def main_kernel(which, spec, sat, wind, cloudy, coll, growth, fall, chosen, edge, *rest):
    result, rim, lhs, coef, stencil = rest[-10:-5] if which == 0 else rest[-9:-4]
    turn, raw, parts, held = rest[-4:]
    if which == 0:
        rest[-5][...] = edge[...]
    begin, end = shares()[which]
    owner = ((iota((1, COLS), 1) + 2) & (COLS - 1)) >> 2

    @pl.when((begin == 0) & (end > 0))
    def _():
        prepare(coll, growth, fall, wind, chosen, lhs, coef, stencil, raw, parts)

    def advect(n):
        t = n >> 1
        b = n & 1
        start = block_row(t, b)
        for l in range(LEV):
            settled = held[l]
            spot = n * LEV + l
            rim[...] = jnp.where(owner == spot, pltpu.roll(settled, 4 * spot, 1), rim[...])
            w = [stencil[k, pl.ds(b * LEV + l, 1), :] for k in range(5)]
            y = w[2] * settled
            for by in (-2, -1, 1, 2):
                y = y + w[by + 2] * pltpu.roll(settled, (COLS - by) % COLS, 1)
            for q in range(4):
                result[pl.ds(start + l + 32 * q, 8, stride=LEV), :] = y[8 * q : 8 * q + 8]
            result[pl.ds(start + l + 128, 1), :] = y[32:33]

    def one(n, carry):
        advect(jnp.maximum(n - 1, begin))
        t = n >> 1
        b = n & 1
        start = block_row(t, b)
        left = lhs[pl.ds(pl.multiple_of(t * MROWS, 16), MROWS), :]
        rate = coef[t]
        speed = coef[TYPES + t]
        wet = cloudy[pl.ds(b, 1), :] > 0
        before = []
        state = []
        for l in range(LEV):
            main = spec[pl.ds(start + l, 32, stride=LEV), :]
            top = spec[pl.ds(start + 128 + l, 1), :]
            before.append((main, top))
            row = sat[pl.ds(b * LEV + l, 1), :]
            state.append(condense(main, top, row, rate[0:32], rate[32:33]))
        for step in range(SUB):
            for half in range(2):
                levels = range(2 * half, 2 * half + 2)
                gain = collect(
                    left,
                    [state[l] for l in levels],
                    [turn.at[LEV * step + l] for l in levels],
                )
                for k in range(2):
                    l = 2 * half + k
                    mine = gain[:, COLS * k : COLS * k + COLS]
                    main, top = state[l]
                    state[l] = (
                        main + (mine[0:32] + mine[40:72]),
                        top + (mine[32:33] + mine[72:73]),
                    )
        above = None
        for l in reversed(range(LEV)):
            main = jnp.where(wet, state[l][0], before[l][0])
            top = jnp.where(wet, state[l][1], before[l][1])
            over = (jnp.zeros_like(main), jnp.zeros_like(top)) if above is None else above
            held[l, 0:32, :] = main + speed[0:32] * (over[0] - main)
            held[l, 32:40, :] = jnp.broadcast_to(top + speed[32:33] * (over[1] - top), (8, COLS))
            above = (main, top)
        return carry

    lax.fori_loop(begin, end, one, 0)

    @pl.when(end > begin)
    def _():
        advect(end - 1)


def finish_kernel(result, rim, from_left, from_right, edge, lhs, coef, out, turn, final, sems):
    lane = iota((1, COLS), 1)
    owner = ((lane + 2) & 127) >> 2
    kind = owner >> 3
    place = lane & 3
    halo = jnp.where(place < 2, from_right[...], from_left[...])

    def by_type(pieces):
        value = pieces[0]
        for t in range(1, TYPES):
            value = jnp.where(kind == t, pieces[t], value)
        return value

    rate = by_type([coef[t] for t in range(TYPES)])
    speed = by_type([coef[TYPES + t] for t in range(TYPES)])
    main = halo[0:32]
    top = halo[32:33]
    wet = halo[35:36] > 0
    state = condense(main, top, halo[33:34], rate[0:32], rate[32:33])
    for step in range(SUB):
        gain = collect_apart(lhs, *state, turn.at[step])
        share = by_type([gain[MROWS * t : MROWS * t + MROWS] for t in range(TYPES)])
        state = (
            state[0] + (share[0:32] + share[40:72]),
            state[1] + (share[32:33] + share[72:73]),
        )
    highest = (owner & 3) == LEV - 1

    def settle(value, speed):
        above = jnp.where(highest, 0.0, pltpu.roll(value, COLS - 4, 1))
        return value + speed * (above - value)

    ghost = jnp.concatenate(
        [
            settle(jnp.where(wet, state[0], main), speed[0:32]),
            settle(jnp.broadcast_to(jnp.where(wet, state[1], top), (8, COLS)), speed[32:40]),
        ],
        axis=0,
    )

    far = jnp.broadcast_to(halo[34:35], (8, COLS))
    near = jnp.broadcast_to(edge[34:35], (8, COLS))
    lower = jnp.where(place == 0, pltpu.roll(far, 1, 1), pltpu.roll(near, 1, 1))
    upper = jnp.where(place == 3, pltpu.roll(far, COLS - 1, 1), pltpu.roll(near, COLS - 1, 1))
    left = (near + lower) * SCALE
    right = (near + upper) * SCALE
    left_abs = jnp.abs(left)
    right_abs = jnp.abs(right)

    def by_place(first, second, third, fourth):
        value = jnp.where(place == 0, first, jnp.where(place == 3, fourth, 0.0))
        return jnp.where(place == 1, second, jnp.where(place == 2, third, value))[0:1]

    own_0 = by_place(7.0 * left + 3.0 * left_abs, 0.0, 0.0, -(7.0 * right - 3.0 * right_abs))
    own_1 = by_place(-(left + left_abs), 0.0, 0.0, right - right_abs)
    halo_1 = by_place(
        (7.0 * left - 3.0 * left_abs) + (right - right_abs),
        0.0,
        0.0,
        -(7.0 * right + 3.0 * right_abs) - (left + left_abs),
    )
    halo_2 = by_place(
        left_abs - left, left_abs - left, right + right_abs, right + right_abs
    )
    inner = rim[...]
    inner_1 = jnp.where(place == 0, pltpu.roll(inner, COLS - 1, 1), pltpu.roll(inner, 1, 1))
    ghost_1 = jnp.where(place == 0, pltpu.roll(ghost, 1, 1), pltpu.roll(ghost, COLS - 1, 1))
    ghost_2 = jnp.where(place < 2, pltpu.roll(ghost, 2, 1), pltpu.roll(ghost, COLS - 2, 1))
    extra = own_0 * inner + own_1 * inner_1 + halo_1 * ghost_1 + halo_2 * ghost_2

    outer = (lane < 2) | (lane >= COLS - 2)
    for b in range(BLK):
        for t in range(TYPES):
            for l in range(LEV):
                spot = (t * BLK + b) * LEV + l
                added = jnp.where(outer, pltpu.roll(extra, (COLS - 4 * spot) % COLS, 1), 0.0)
                start = block_row(t, b) + l
                for q in range(4):
                    rows = pl.ds(start + 32 * q, 8, stride=LEV)
                    final[rows, :] = result[rows, :] + added[8 * q : 8 * q + 8]
                rows = slice(start + 128, start + 129)
                final[rows, :] = result[rows, :] + added[32:33]
        rows = pl.ds(b * (ROWS // BLK), ROWS // BLK)
        pltpu.make_async_copy(final.at[rows], out.at[rows], sems.at[b]).start()
    for b in range(BLK):
        rows = pl.ds(b * (ROWS // BLK), ROWS // BLK)
        pltpu.make_async_copy(final.at[rows], out.at[rows], sems.at[b]).wait()


def vmem(count):
    return [pl.BlockSpec(memory_space=pltpu.VMEM)] * count


def resident(*arrays):
    return [pltpu.with_memory_space_constraint(x, pltpu.VMEM) for x in arrays]


def body(spectra, collection, growth_rate, fall_speed, supersaturation, courant, cloudy):
    sources = (
        spectra.reshape(ROWS, COLS),
        supersaturation.reshape(BLK * LEV, COLS),
        courant.reshape(BLK * LEV, COLS),
        cloudy,
        jnp.transpose(collection, (1, 0, 2)),
        growth_rate,
        fall_speed,
    )
    edge, chosen, spec, sat, wind, wet, coll, growth, fall = pl.pallas_call(
        edge_kernel,
        out_shape=(
            pltpu.VMEM((40, COLS), F32),
            pltpu.VMEM((KDIM, KDIM), BF16),
            *(pltpu.VMEM(x.shape, x.dtype) for x in sources),
        ),
        in_specs=[pl.BlockSpec(memory_space=pl.ANY)] * len(sources),
        out_specs=tuple(vmem(2 + len(sources))),
        scratch_shapes=[pltpu.SemaphoreType.DMA((1 + len(sources),))],
        name="edges",
    )(*sources)

    def blocks(which, edge, held):
        shapes = (
            pltpu.VMEM((ROWS, COLS), F32),
            pltpu.VMEM((40, COLS), F32),
            pltpu.VMEM((TYPES * MROWS, KDIM), BF16),
            pltpu.VMEM((2 * TYPES, 40, COLS), F32),
            pltpu.VMEM((5, BLK * LEV, COLS), F32),
        )
        if which == 0:
            shapes += (pltpu.VMEM((40, COLS), F32),)
        return pl.pallas_call(
            lambda *refs: main_kernel(which, *refs),
            out_shape=shapes,
            in_specs=vmem(9 + len(held)),
            out_specs=tuple(vmem(len(shapes))),
            input_output_aliases={9 + n: n for n in range(len(held))},
            scratch_shapes=[
                pltpu.VMEM((SUB * LEV, 48, COLS), F32),
                pltpu.VMEM((KDIM // COLS, TYPES * 40, COLS), F32),
                pltpu.VMEM((TYPES * MROWS, KDIM), BF16),
                pltpu.VMEM((LEV, 40, COLS), F32),
            ],
        )(*resident(spec, sat, wind, wet, coll, growth, fall, chosen, edge, *held))

    count = lax.axis_size("gy")
    up = [(i, (i + 1) % count) for i in range(count)]
    down = [(j, i) for i, j in up]
    *held, packed = blocks(0, edge, ())
    from_left = lax.ppermute(packed, "gy", up)
    from_right = lax.ppermute(packed, "gy", down)
    result, rim, lhs, coef, _ = blocks(1, packed, held)
    out = pl.pallas_call(
        finish_kernel,
        out_shape=jax.ShapeDtypeStruct((ROWS, COLS), F32),
        in_specs=vmem(7),
        out_specs=pl.BlockSpec(memory_space=pl.ANY),
        scratch_shapes=[
            pltpu.VMEM((SUB, 48, COLS), F32),
            pltpu.VMEM((ROWS, COLS), F32),
            pltpu.SemaphoreType.DMA((BLK,)),
        ],
        name="finish",
    )(*resident(result, rim, from_left, from_right, edge, lhs, coef))
    return out.reshape(spectra.shape)


def solution(mesh):
    return jax.shard_map(
        body,
        mesh=mesh,
        in_specs=(
            P("gx", None, None, None, "gy"),
            P(),
            P(),
            P(),
            P("gx", None, "gy"),
            P("gx", None, "gy"),
            P("gx", "gy"),
        ),
        out_specs=P("gx", None, None, None, "gy"),
        check_vma=False,
    )
```

```python
import jax
import jax.numpy as jnp
from jax import lax
from jax.experimental import pallas as pl
from jax.experimental.pallas import tpu as pltpu
from jax.sharding import PartitionSpec as P


TYPES = 4
BINS = 33
LEV = 4
BLK = 2
SUB = 2
COLS = 128
ROWS = BLK * TYPES * BINS * LEV
PAIRS = BINS * (BINS + 1) // 2
HALF = 512
TAIL = 64
KDIM = HALF + 2 * TAIL
MROWS = 80
SCALE = 0.5 / 12.0
LIMIT = 16 << 20
F32 = jnp.float32
BF16 = jnp.bfloat16


def iota(shape, axis):
    return lax.broadcasted_iota(jnp.int32, shape, axis)


def split(x):
    high = x.astype(BF16)
    low = (x - high.astype(F32)).astype(BF16)
    return high, low


def block_row(t, b):
    return (b * TYPES + t) * BINS * LEV


def pair_of_column(col):
    tail = jnp.where(col >= HALF + TAIL, col - TAIL, col)
    first = jnp.where(col < HALF, col & 31, jnp.where(tail < 528, tail - HALF, tail - 528))
    second = jnp.where(
        col < HALF, (first + (col >> 5)) & 31, jnp.where(tail < 528, first + 16, BINS - 1)
    )
    low = jnp.minimum(first, second)
    high = jnp.maximum(first, second)
    pair = low * BINS - ((low * (low - 1)) >> 1) + (high - low)
    return jnp.where(tail > 560, -1, pair)


def edge_kernel(*refs):
    sources, edge, chosen, kept, sems = refs[:7], refs[7], refs[8], refs[9:16], refs[16]
    halves = [pl.ds(b * (ROWS // BLK), ROWS // BLK) for b in range(BLK)]
    pairs = [(sources[0].at[rows], kept[0].at[rows]) for rows in halves]
    pairs += list(zip(sources[1:], kept[1:]))
    copies = [pltpu.make_async_copy(*pair, sems.at[n]) for n, pair in enumerate(pairs)]
    for n in (2, 3, 4, 0, 1, 5, 6, 7):
        copies[n].start()
    wanted = pair_of_column(iota((1, KDIM), 1))
    for first in range(0, KDIM, COLS):
        rows = iota((COLS, KDIM), 0) + first
        chosen[first : first + COLS, :] = jnp.where(rows == wanted, 1.0, 0.0).astype(BF16)
    spec, sat, wind, cloudy = kept[:4]
    for copy in copies[2:5]:
        copy.wait()
    lane = iota((1, COLS), 1)
    owner = ((lane + 2) & 127) >> 2
    row8 = iota((8, COLS), 0)
    main = [jnp.zeros((8, COLS), F32) for _ in range(4)]
    last = jnp.zeros((8, COLS), F32)
    for b in range(BLK):
        copies[b].wait()
        cloud_row = cloudy[b : b + 1, :].astype(F32)
        for l in range(LEV):
            extra = jnp.where(
                row8 == 1,
                sat[b * LEV + l : b * LEV + l + 1, :],
                jnp.where(row8 == 2, wind[b * LEV + l : b * LEV + l + 1, :], cloud_row),
            )
            for t in range(TYPES):
                spot = (t * BLK + b) * LEV + l
                mine = owner == spot
                start = block_row(t, b) + l
                for q in range(4):
                    piece = spec[pl.ds(start + 32 * q, 8, stride=LEV), :]
                    main[q] = jnp.where(mine, pltpu.roll(piece, 4 * spot, 1), main[q])
                piece = jnp.where(row8 == 0, spec[start + 128 : start + 129, :], extra)
                last = jnp.where(mine, pltpu.roll(piece, 4 * spot, 1), last)
    for q in range(4):
        edge[8 * q : 8 * q + 8, :] = main[q]
    edge[32:40, :] = last
    for copy in copies[5:]:
        copy.wait()


def weights(left, right):
    left_abs = jnp.abs(left)
    right_abs = jnp.abs(right)
    return (
        left_abs - left,
        (right - right_abs) + (7.0 * left - 3.0 * left_abs),
        1.0 - (7.0 * right - 3.0 * right_abs) + (7.0 * left + 3.0 * left_abs),
        -(7.0 * right + 3.0 * right_abs) - (left + left_abs),
        right + right_abs,
    )


def prepare(coll, growth, fall, wind, chosen, lhs, coef, stencil, raw, parts):
    stacked = jnp.concatenate(
        [
            jnp.concatenate([growth[...], fall[...]], axis=0),
            jnp.zeros((COLS - 2 * TYPES, BINS), F32),
        ],
        axis=0,
    )
    stacked = jnp.concatenate([stacked, jnp.zeros((COLS, COLS - BINS), F32)], axis=1)
    turned = jnp.transpose(stacked)[0:40, :]
    for n in range(2 * TYPES):
        coef[n] = jnp.broadcast_to(turned[:, n : n + 1], (40, COLS))
    lane = iota((1, COLS), 1)
    own = wind[...]
    left = jnp.where(lane == 0, 0.0, (own + pltpu.roll(own, 1, 1)) * SCALE)
    right = jnp.where(lane == COLS - 1, 0.0, (own + pltpu.roll(own, COLS - 1, 1)) * SCALE)
    for by, value in zip(range(-2, 3), weights(left, right)):
        inside = (lane + by >= 0) & (lane + by < COLS)
        stencil[by + 2] = jnp.where(inside, value, 0.0)
    raw[...] = jnp.zeros(raw.shape, F32)
    for n in range(KDIM // COLS):
        width = min(COLS, PAIRS - COLS * n)
        for k in range(BINS):
            raw[n, TYPES * k : TYPES * k + TYPES, 0:width] = coll[k, :, COLS * n : COLS * n + width]
    for t in range(TYPES):
        for n in range(KDIM // COLS):
            rows = raw[n, pl.ds(t, 40, stride=TYPES), :]
            both = jnp.concatenate(split(rows), axis=0)
            parts[MROWS * t : MROWS * t + MROWS, COLS * n : COLS * n + COLS] = both
    lhs[...] = jnp.dot(parts[...], chosen[...], preferred_element_type=F32).astype(BF16)


def condense(main, top, sat, rate_main, rate_top):
    rising = jnp.maximum(sat, 0.0)
    falling = jnp.maximum(-sat, 0.0)
    transfer = rate_main * main
    up = rising * transfer
    down = falling * transfer
    down_top = falling * (rate_top * top)
    arrive_up = jnp.concatenate([jnp.zeros_like(top), up[:-1]], axis=0)
    arrive_down = jnp.concatenate([down[1:], down_top], axis=0)
    new_main = main - up - down + arrive_up + arrive_down
    new_top = top - down_top + up[-1:]
    return new_main, new_top


def pair_parts(groups, turns):
    for (main, top), turn in zip(groups, turns):
        turn[0:32, :] = main
        turn[32:48, :] = main[0:16]

    def gather(pieces):
        return jnp.concatenate(pieces, axis=1) if len(pieces) > 1 else pieces[0]

    for first in range(0, 16, 4):
        tiles = []
        for (main, _), turn in zip(groups, turns):
            parts = [
                split(main * (main if d == 0 else turn[d : d + 32, :]))
                for d in range(first, first + 4)
            ]
            tiles.append(jnp.concatenate([p[0] for p in parts] + [p[1] for p in parts], axis=0))
        columns = slice(32 * first, 32 * first + 128)
        yield (columns, columns), gather(tiles)
    tails = []
    for main, top in groups:
        square = jnp.where(iota((16, COLS), 0) == 0, top * top, 0.0)
        rest = jnp.concatenate([main[0:16] * main[16:32], main * top, square], axis=0)
        tails.append(jnp.concatenate(split(rest), axis=0))
    yield (slice(HALF, KDIM),), gather(tails)


def collect(lhs, groups, turns):
    total = None
    for columns, part in pair_parts(groups, turns):
        gain = jnp.dot(
            jnp.concatenate([lhs[:, c] for c in columns], axis=1), part, preferred_element_type=F32
        )
        total = gain if total is None else total + gain
    return total


def collect_apart(lhs, main, top, turn):
    turn[0:32, :] = main
    turn[32:48, :] = main[0:16]
    total = None
    for first in range(0, 16, 8):
        value = jnp.concatenate(
            [main * (main if d == 0 else turn[d : d + 32, :]) for d in range(first, first + 8)],
            axis=0,
        )
        part = jnp.concatenate(split(value), axis=1)
        gain = jnp.dot(lhs[:, 32 * first : 32 * first + 256], part, preferred_element_type=F32)
        total = gain if total is None else total + gain
    square = jnp.where(iota((16, COLS), 0) == 0, top * top, 0.0)
    rest = jnp.concatenate([main[0:16] * main[16:32], main * top, square], axis=0)
    part = jnp.concatenate(split(rest), axis=1)
    total = total + jnp.dot(lhs[:, HALF : HALF + TAIL], part, preferred_element_type=F32)
    return total[:, 0:COLS] + total[:, COLS : 2 * COLS]


def shares():
    x, y = lax.axis_index("gx"), lax.axis_index("gy")
    z = y >> 1
    first = jnp.int32(0)
    for n, count in enumerate((8, 7, 5, 3, 1)):
        first = jnp.where(z == n, count, first)
    first = jnp.where((x == 0) & (y == 0), 0, first)
    return (0, first), (first, BLK * TYPES)


def main_kernel(which, spec, sat, wind, cloudy, coll, growth, fall, chosen, edge, *rest):
    result, rim, lhs, coef, stencil = rest[-10:-5] if which == 0 else rest[-9:-4]
    turn, raw, parts, held = rest[-4:]
    if which == 0:
        rest[-5][...] = edge[...]
    begin, end = shares()[which]
    owner = ((iota((1, COLS), 1) + 2) & (COLS - 1)) >> 2

    @pl.when((begin == 0) & (end > 0))
    def _():
        prepare(coll, growth, fall, wind, chosen, lhs, coef, stencil, raw, parts)

    def advect(n):
        t = n >> 1
        b = n & 1
        start = block_row(t, b)
        for l in range(LEV):
            settled = held[l]
            spot = n * LEV + l
            rim[...] = jnp.where(owner == spot, pltpu.roll(settled, 4 * spot, 1), rim[...])
            w = [stencil[k, pl.ds(b * LEV + l, 1), :] for k in range(5)]
            y = w[2] * settled
            for by in (-2, -1, 1, 2):
                y = y + w[by + 2] * pltpu.roll(settled, (COLS - by) % COLS, 1)
            for q in range(4):
                result[pl.ds(start + l + 32 * q, 8, stride=LEV), :] = y[8 * q : 8 * q + 8]
            result[pl.ds(start + l + 128, 1), :] = y[32:33]

    def one(n, carry):
        advect(jnp.maximum(n - 1, begin))
        t = n >> 1
        b = n & 1
        start = block_row(t, b)
        left = lhs[pl.ds(pl.multiple_of(t * MROWS, 16), MROWS), :]
        rate = coef[t]
        speed = coef[TYPES + t]
        wet = cloudy[pl.ds(b, 1), :] > 0
        before = []
        state = []
        for l in range(LEV):
            main = spec[pl.ds(start + l, 32, stride=LEV), :]
            top = spec[pl.ds(start + 128 + l, 1), :]
            before.append((main, top))
            row = sat[pl.ds(b * LEV + l, 1), :]
            state.append(condense(main, top, row, rate[0:32], rate[32:33]))
        for step in range(SUB):
            for half in range(2):
                levels = range(2 * half, 2 * half + 2)
                gain = collect(
                    left,
                    [state[l] for l in levels],
                    [turn.at[LEV * step + l] for l in levels],
                )
                for k in range(2):
                    l = 2 * half + k
                    mine = gain[:, COLS * k : COLS * k + COLS]
                    main, top = state[l]
                    state[l] = (
                        main + (mine[0:32] + mine[40:72]),
                        top + (mine[32:33] + mine[72:73]),
                    )
        above = None
        for l in reversed(range(LEV)):
            main = jnp.where(wet, state[l][0], before[l][0])
            top = jnp.where(wet, state[l][1], before[l][1])
            over = (jnp.zeros_like(main), jnp.zeros_like(top)) if above is None else above
            held[l, 0:32, :] = main + speed[0:32] * (over[0] - main)
            held[l, 32:40, :] = jnp.broadcast_to(top + speed[32:33] * (over[1] - top), (8, COLS))
            above = (main, top)
        return carry

    lax.fori_loop(begin, end, one, 0)

    @pl.when(end > begin)
    def _():
        advect(end - 1)


def finish_kernel(result, rim, from_left, from_right, edge, lhs, coef, out, turn, final, sems):
    lane = iota((1, COLS), 1)
    owner = ((lane + 2) & 127) >> 2
    kind = owner >> 3
    place = lane & 3
    halo = jnp.where(place < 2, from_right[...], from_left[...])

    def by_type(pieces):
        value = pieces[0]
        for t in range(1, TYPES):
            value = jnp.where(kind == t, pieces[t], value)
        return value

    rate = by_type([coef[t] for t in range(TYPES)])
    speed = by_type([coef[TYPES + t] for t in range(TYPES)])
    main = halo[0:32]
    top = halo[32:33]
    wet = halo[35:36] > 0
    state = condense(main, top, halo[33:34], rate[0:32], rate[32:33])
    for step in range(SUB):
        gain = collect_apart(lhs, *state, turn.at[step])
        share = by_type([gain[MROWS * t : MROWS * t + MROWS] for t in range(TYPES)])
        state = (
            state[0] + (share[0:32] + share[40:72]),
            state[1] + (share[32:33] + share[72:73]),
        )
    highest = (owner & 3) == LEV - 1

    def settle(value, speed):
        above = jnp.where(highest, 0.0, pltpu.roll(value, COLS - 4, 1))
        return value + speed * (above - value)

    ghost = jnp.concatenate(
        [
            settle(jnp.where(wet, state[0], main), speed[0:32]),
            settle(jnp.broadcast_to(jnp.where(wet, state[1], top), (8, COLS)), speed[32:40]),
        ],
        axis=0,
    )

    far = jnp.broadcast_to(halo[34:35], (8, COLS))
    near = jnp.broadcast_to(edge[34:35], (8, COLS))
    lower = jnp.where(place == 0, pltpu.roll(far, 1, 1), pltpu.roll(near, 1, 1))
    upper = jnp.where(place == 3, pltpu.roll(far, COLS - 1, 1), pltpu.roll(near, COLS - 1, 1))
    left = (near + lower) * SCALE
    right = (near + upper) * SCALE
    left_abs = jnp.abs(left)
    right_abs = jnp.abs(right)

    def by_place(first, second, third, fourth):
        value = jnp.where(place == 0, first, jnp.where(place == 3, fourth, 0.0))
        return jnp.where(place == 1, second, jnp.where(place == 2, third, value))[0:1]

    own_0 = by_place(7.0 * left + 3.0 * left_abs, 0.0, 0.0, -(7.0 * right - 3.0 * right_abs))
    own_1 = by_place(-(left + left_abs), 0.0, 0.0, right - right_abs)
    halo_1 = by_place(
        (7.0 * left - 3.0 * left_abs) + (right - right_abs),
        0.0,
        0.0,
        -(7.0 * right + 3.0 * right_abs) - (left + left_abs),
    )
    halo_2 = by_place(
        left_abs - left, left_abs - left, right + right_abs, right + right_abs
    )
    inner = rim[...]
    inner_1 = jnp.where(place == 0, pltpu.roll(inner, COLS - 1, 1), pltpu.roll(inner, 1, 1))
    ghost_1 = jnp.where(place == 0, pltpu.roll(ghost, 1, 1), pltpu.roll(ghost, COLS - 1, 1))
    ghost_2 = jnp.where(place < 2, pltpu.roll(ghost, 2, 1), pltpu.roll(ghost, COLS - 2, 1))
    extra = own_0 * inner + own_1 * inner_1 + halo_1 * ghost_1 + halo_2 * ghost_2

    outer = (lane < 2) | (lane >= COLS - 2)
    pieces = [pl.ds(BINS * LEV * n, BINS * LEV) for n in range(BLK * TYPES)]
    copies = [
        pltpu.make_async_copy(final.at[rows], out.at[rows], sems.at[n])
        for n, rows in enumerate(pieces)
    ]
    for b in range(BLK):
        for t in range(TYPES):
            for l in range(LEV):
                spot = (t * BLK + b) * LEV + l
                added = jnp.where(outer, pltpu.roll(extra, (COLS - 4 * spot) % COLS, 1), 0.0)
                start = block_row(t, b) + l
                for q in range(4):
                    rows = pl.ds(start + 32 * q, 8, stride=LEV)
                    final[rows, :] = result[rows, :] + added[8 * q : 8 * q + 8]
                rows = slice(start + 128, start + 129)
                final[rows, :] = result[rows, :] + added[32:33]
            copies[b * TYPES + t].start()
    for copy in copies:
        copy.wait()


def vmem(count):
    return [pl.BlockSpec(memory_space=pltpu.VMEM)] * count


def placed(space, *arrays):
    return [pltpu.with_memory_space_constraint(x, space) for x in arrays]


def resident(*arrays):
    return placed(pltpu.VMEM, *arrays)


def body(spectra, collection, growth_rate, fall_speed, supersaturation, courant, cloudy):
    sources = (
        spectra.reshape(ROWS, COLS),
        supersaturation.reshape(BLK * LEV, COLS),
        courant.reshape(BLK * LEV, COLS),
        cloudy,
        jnp.transpose(collection, (1, 0, 2)),
        growth_rate,
        fall_speed,
    )
    edge, chosen, spec, sat, wind, wet, coll, growth, fall = pl.pallas_call(
        edge_kernel,
        out_shape=(
            pltpu.VMEM((40, COLS), F32),
            pltpu.VMEM((KDIM, KDIM), BF16),
            *(pltpu.VMEM(x.shape, x.dtype) for x in sources),
        ),
        in_specs=[pl.BlockSpec(memory_space=pltpu.HBM)] * len(sources),
        out_specs=tuple(vmem(2 + len(sources))),
        scratch_shapes=[pltpu.SemaphoreType.DMA((1 + len(sources),))],
        compiler_params=pltpu.CompilerParams(vmem_limit_bytes=LIMIT),
        name="edges",
    )(*placed(pltpu.HBM, *sources))

    def blocks(which, edge, held):
        shapes = (
            pltpu.VMEM((ROWS, COLS), F32),
            pltpu.VMEM((40, COLS), F32),
            pltpu.VMEM((TYPES * MROWS, KDIM), BF16),
            pltpu.VMEM((2 * TYPES, 40, COLS), F32),
            pltpu.VMEM((5, BLK * LEV, COLS), F32),
        )
        if which == 0:
            shapes += (pltpu.VMEM((40, COLS), F32),)
        return pl.pallas_call(
            lambda *refs: main_kernel(which, *refs),
            out_shape=shapes,
            in_specs=vmem(9 + len(held)),
            out_specs=tuple(vmem(len(shapes))),
            input_output_aliases={9 + n: n for n in range(len(held))},
            scratch_shapes=[
                pltpu.VMEM((SUB * LEV, 48, COLS), F32),
                pltpu.VMEM((KDIM // COLS, TYPES * 40, COLS), F32),
                pltpu.VMEM((TYPES * MROWS, KDIM), BF16),
                pltpu.VMEM((LEV, 40, COLS), F32),
            ],
            compiler_params=pltpu.CompilerParams(vmem_limit_bytes=LIMIT),
        )(*resident(spec, sat, wind, wet, coll, growth, fall, chosen, edge, *held))

    count = lax.axis_size("gy")
    up = [(i, (i + 1) % count) for i in range(count)]
    down = [(j, i) for i, j in up]
    *held, packed = blocks(0, edge, ())
    from_left = lax.ppermute(packed, "gy", up)
    from_right = lax.ppermute(packed, "gy", down)
    result, rim, lhs, coef, _ = blocks(1, packed, held)
    out = pl.pallas_call(
        finish_kernel,
        out_shape=jax.ShapeDtypeStruct((ROWS, COLS), F32),
        in_specs=vmem(7),
        out_specs=pl.BlockSpec(memory_space=pl.ANY),
        scratch_shapes=[
            pltpu.VMEM((SUB, 48, COLS), F32),
            pltpu.VMEM((ROWS, COLS), F32),
            pltpu.SemaphoreType.DMA((BLK * TYPES,)),
        ],
        compiler_params=pltpu.CompilerParams(vmem_limit_bytes=LIMIT),
        name="finish",
    )(*resident(result, rim, from_left, from_right, edge, lhs, coef))
    return out.reshape(spectra.shape)


def solution(mesh):
    return jax.shard_map(
        body,
        mesh=mesh,
        in_specs=(
            P("gx", None, None, None, "gy"),
            P(),
            P(),
            P(),
            P("gx", None, "gy"),
            P("gx", None, "gy"),
            P("gx", "gy"),
        ),
        out_specs=P("gx", None, None, None, "gy"),
        check_vma=False,
    )
```

```python
import jax
import jax.numpy as jnp
from jax import lax
from jax.experimental import pallas as pl
from jax.experimental.pallas import tpu as pltpu
from jax.sharding import PartitionSpec as P


TYPES = 4
BINS = 33
LEV = 4
BLK = 2
SUB = 2
COLS = 128
ROWS = BLK * TYPES * BINS * LEV
PAIRS = BINS * (BINS + 1) // 2
HALF = 512
TAIL = 64
KDIM = HALF + 2 * TAIL
MROWS = 80
SCALE = 0.5 / 12.0
LIMIT = 16 << 20
F32 = jnp.float32
BF16 = jnp.bfloat16


def iota(shape, axis):
    return lax.broadcasted_iota(jnp.int32, shape, axis)


def split(x):
    high = x.astype(BF16)
    low = (x - high.astype(F32)).astype(BF16)
    return high, low


def block_row(t, b):
    return (b * TYPES + t) * BINS * LEV


def pair_of_column(col):
    tail = jnp.where(col >= HALF + TAIL, col - TAIL, col)
    first = jnp.where(col < HALF, col & 31, jnp.where(tail < 528, tail - HALF, tail - 528))
    second = jnp.where(
        col < HALF, (first + (col >> 5)) & 31, jnp.where(tail < 528, first + 16, BINS - 1)
    )
    low = jnp.minimum(first, second)
    high = jnp.maximum(first, second)
    pair = low * BINS - ((low * (low - 1)) >> 1) + (high - low)
    return jnp.where(tail > 560, -1, pair)


def edge_kernel(*refs):
    sources, edge, chosen, kept, sems = refs[:7], refs[7], refs[8], refs[9:16], refs[16]
    halves = [pl.ds(b * (ROWS // BLK), ROWS // BLK) for b in range(BLK)]
    pairs = [(sources[0].at[rows], kept[0].at[rows]) for rows in halves]
    pairs += list(zip(sources[1:], kept[1:]))
    copies = [pltpu.make_async_copy(*pair, sems.at[n]) for n, pair in enumerate(pairs)]
    for n in (2, 3, 4, 0, 1, 5, 6, 7):
        copies[n].start()
    wanted = pair_of_column(iota((1, KDIM), 1))
    for first in range(0, KDIM, COLS):
        rows = iota((COLS, KDIM), 0) + first
        chosen[first : first + COLS, :] = jnp.where(rows == wanted, 1.0, 0.0).astype(BF16)
    spec, sat, wind, cloudy = kept[:4]
    for copy in copies[2:5]:
        copy.wait()
    lane = iota((1, COLS), 1)
    owner = ((lane + 2) & 127) >> 2
    row8 = iota((8, COLS), 0)
    main = [jnp.zeros((8, COLS), F32) for _ in range(4)]
    last = jnp.zeros((8, COLS), F32)
    for b in range(BLK):
        copies[b].wait()
        cloud_row = cloudy[b : b + 1, :].astype(F32)
        for l in range(LEV):
            extra = jnp.where(
                row8 == 1,
                sat[b * LEV + l : b * LEV + l + 1, :],
                jnp.where(row8 == 2, wind[b * LEV + l : b * LEV + l + 1, :], cloud_row),
            )
            for t in range(TYPES):
                spot = (t * BLK + b) * LEV + l
                mine = owner == spot
                start = block_row(t, b) + l
                for q in range(4):
                    piece = spec[pl.ds(start + 32 * q, 8, stride=LEV), :]
                    main[q] = jnp.where(mine, pltpu.roll(piece, 4 * spot, 1), main[q])
                piece = jnp.where(row8 == 0, spec[start + 128 : start + 129, :], extra)
                last = jnp.where(mine, pltpu.roll(piece, 4 * spot, 1), last)
    for q in range(4):
        edge[8 * q : 8 * q + 8, :] = main[q]
    edge[32:40, :] = last
    for copy in copies[5:]:
        copy.wait()


def weights(left, right):
    left_abs = jnp.abs(left)
    right_abs = jnp.abs(right)
    return (
        left_abs - left,
        (right - right_abs) + (7.0 * left - 3.0 * left_abs),
        1.0 - (7.0 * right - 3.0 * right_abs) + (7.0 * left + 3.0 * left_abs),
        -(7.0 * right + 3.0 * right_abs) - (left + left_abs),
        right + right_abs,
    )


def prepare(coll, growth, fall, wind, chosen, lhs, coef, stencil, raw, parts):
    stacked = jnp.concatenate(
        [
            jnp.concatenate([growth[...], fall[...]], axis=0),
            jnp.zeros((COLS - 2 * TYPES, BINS), F32),
        ],
        axis=0,
    )
    stacked = jnp.concatenate([stacked, jnp.zeros((COLS, COLS - BINS), F32)], axis=1)
    turned = jnp.transpose(stacked)[0:40, :]
    for n in range(2 * TYPES):
        coef[n] = jnp.broadcast_to(turned[:, n : n + 1], (40, COLS))
    lane = iota((1, COLS), 1)
    own = wind[...]
    left = jnp.where(lane == 0, 0.0, (own + pltpu.roll(own, 1, 1)) * SCALE)
    right = jnp.where(lane == COLS - 1, 0.0, (own + pltpu.roll(own, COLS - 1, 1)) * SCALE)
    for by, value in zip(range(-2, 3), weights(left, right)):
        inside = (lane + by >= 0) & (lane + by < COLS)
        stencil[by + 2] = jnp.where(inside, value, 0.0)
    raw[KDIM // COLS - 1] = jnp.zeros(raw.shape[1:], F32)
    for n in range(KDIM // COLS):
        width = min(COLS, PAIRS - COLS * n)
        for k in range(BINS):
            raw[n, TYPES * k : TYPES * k + TYPES, 0:width] = coll[k, :, COLS * n : COLS * n + width]
    for t in range(TYPES):
        for n in range(KDIM // COLS):
            rows = raw[n, pl.ds(t, 40, stride=TYPES), :]
            both = jnp.concatenate(split(rows), axis=0)
            parts[MROWS * t : MROWS * t + MROWS, COLS * n : COLS * n + COLS] = both
    lhs[...] = jnp.dot(parts[...], chosen[...], preferred_element_type=F32).astype(BF16)


def condense(main, top, sat, rate_main, rate_top):
    rising = jnp.maximum(sat, 0.0)
    falling = jnp.maximum(-sat, 0.0)
    transfer = rate_main * main
    up = rising * transfer
    down = falling * transfer
    down_top = falling * (rate_top * top)
    arrive_up = jnp.concatenate([jnp.zeros_like(top), up[:-1]], axis=0)
    arrive_down = jnp.concatenate([down[1:], down_top], axis=0)
    new_main = main - up - down + arrive_up + arrive_down
    new_top = top - down_top + up[-1:]
    return new_main, new_top


def pair_parts(groups, turns):
    for (main, top), turn in zip(groups, turns):
        turn[0:32, :] = main
        turn[32:48, :] = main[0:16]

    def gather(pieces):
        return jnp.concatenate(pieces, axis=1) if len(pieces) > 1 else pieces[0]

    for first in range(0, 16, 4):
        tiles = []
        for (main, _), turn in zip(groups, turns):
            parts = [
                split(main * (main if d == 0 else turn[d : d + 32, :]))
                for d in range(first, first + 4)
            ]
            tiles.append(jnp.concatenate([p[0] for p in parts] + [p[1] for p in parts], axis=0))
        columns = slice(32 * first, 32 * first + 128)
        yield (columns, columns), gather(tiles)
    tails = []
    for main, top in groups:
        square = jnp.where(iota((16, COLS), 0) == 0, top * top, 0.0)
        rest = jnp.concatenate([main[0:16] * main[16:32], main * top, square], axis=0)
        tails.append(jnp.concatenate(split(rest), axis=0))
    yield (slice(HALF, KDIM),), gather(tails)


def collect(lhs, groups, turns):
    total = None
    for columns, part in pair_parts(groups, turns):
        gain = jnp.dot(
            jnp.concatenate([lhs[:, c] for c in columns], axis=1), part, preferred_element_type=F32
        )
        total = gain if total is None else total + gain
    return total


def collect_apart(lhs, main, top, turn):
    turn[0:32, :] = main
    turn[32:48, :] = main[0:16]
    total = None
    for first in range(0, 16, 8):
        value = jnp.concatenate(
            [main * (main if d == 0 else turn[d : d + 32, :]) for d in range(first, first + 8)],
            axis=0,
        )
        part = jnp.concatenate(split(value), axis=1)
        gain = jnp.dot(lhs[:, 32 * first : 32 * first + 256], part, preferred_element_type=F32)
        total = gain if total is None else total + gain
    square = jnp.where(iota((16, COLS), 0) == 0, top * top, 0.0)
    rest = jnp.concatenate([main[0:16] * main[16:32], main * top, square], axis=0)
    part = jnp.concatenate(split(rest), axis=1)
    total = total + jnp.dot(lhs[:, HALF : HALF + TAIL], part, preferred_element_type=F32)
    return total[:, 0:COLS] + total[:, COLS : 2 * COLS]


UP = ((6, 4, 3, 1, 0, 0, 0, 0), (7, 5, 4, 2, 1, 1, 1, 0))
DOWN = ((8, 5, 4, 2, 1, 1, 1, 0), (7, 5, 4, 2, 1, 1, 1, 0))


def shares():
    x, y = lax.axis_index("gx"), lax.axis_index("gy")

    def pick(table):
        value = jnp.int32(0)
        for odd in range(2):
            for z, count in enumerate(table[odd]):
                value = jnp.where(y == 2 * z + odd, count, value)
        return value

    origin = (x == 0) & (y == 0)
    first = jnp.where(origin, 0, pick(UP))
    second = jnp.where(origin, 1, pick(DOWN))
    ahead = ((x == 0) & (y == 2)).astype(jnp.int32)
    first, second = first - ahead, second - ahead
    return (0, first), (first, second), (second, BLK * TYPES)


def main_kernel(which, spec, sat, wind, cloudy, coll, growth, fall, chosen, edge, *rest):
    result, rim, lhs, coef, stencil = rest[-10:-5] if which < 2 else rest[-9:-4]
    turn, raw, parts, held = rest[-4:]
    if which < 2:
        rest[-5][...] = edge[...]
    begin, end = shares()[which]
    owner = ((iota((1, COLS), 1) + 2) & (COLS - 1)) >> 2

    @pl.when((begin == 0) & (end > 0))
    def _():
        prepare(coll, growth, fall, wind, chosen, lhs, coef, stencil, raw, parts)

    def advect(n):
        t = n >> 1
        b = n & 1
        start = block_row(t, b)
        for l in range(LEV):
            settled = held[l]
            spot = n * LEV + l
            rim[...] = jnp.where(owner == spot, pltpu.roll(settled, 4 * spot, 1), rim[...])
            w = [stencil[k, pl.ds(b * LEV + l, 1), :] for k in range(5)]
            y = w[2] * settled
            for by in (-2, -1, 1, 2):
                y = y + w[by + 2] * pltpu.roll(settled, (COLS - by) % COLS, 1)
            for q in range(4):
                result[pl.ds(start + l + 32 * q, 8, stride=LEV), :] = y[8 * q : 8 * q + 8]
            result[pl.ds(start + l + 128, 1), :] = y[32:33]

    def one(n, carry):
        advect(jnp.maximum(n - 1, begin))
        t = n >> 1
        b = n & 1
        start = block_row(t, b)
        left = lhs[pl.ds(pl.multiple_of(t * MROWS, 16), MROWS), :]
        rate = coef[t]
        speed = coef[TYPES + t]
        wet = cloudy[pl.ds(b, 1), :] > 0
        before = []
        state = []
        for l in range(LEV):
            main = spec[pl.ds(start + l, 32, stride=LEV), :]
            top = spec[pl.ds(start + 128 + l, 1), :]
            before.append((main, top))
            row = sat[pl.ds(b * LEV + l, 1), :]
            state.append(condense(main, top, row, rate[0:32], rate[32:33]))
        for step in range(SUB):
            for half in range(2):
                levels = range(2 * half, 2 * half + 2)
                gain = collect(
                    left,
                    [state[l] for l in levels],
                    [turn.at[LEV * step + l] for l in levels],
                )
                for k in range(2):
                    l = 2 * half + k
                    mine = gain[:, COLS * k : COLS * k + COLS]
                    main, top = state[l]
                    state[l] = (
                        main + (mine[0:32] + mine[40:72]),
                        top + (mine[32:33] + mine[72:73]),
                    )
        above = None
        for l in reversed(range(LEV)):
            main = jnp.where(wet, state[l][0], before[l][0])
            top = jnp.where(wet, state[l][1], before[l][1])
            over = (jnp.zeros_like(main), jnp.zeros_like(top)) if above is None else above
            held[l, 0:32, :] = main + speed[0:32] * (over[0] - main)
            held[l, 32:40, :] = jnp.broadcast_to(top + speed[32:33] * (over[1] - top), (8, COLS))
            above = (main, top)
        return carry

    lax.fori_loop(begin, end, one, 0)

    @pl.when(end > begin)
    def _():
        advect(end - 1)


def finish_kernel(result, rim, from_left, from_right, edge, lhs, coef, out, turn, final, sems):
    lane = iota((1, COLS), 1)
    owner = ((lane + 2) & 127) >> 2
    kind = owner >> 3
    place = lane & 3
    halo = jnp.where(place < 2, from_right[...], from_left[...])

    def by_type(pieces):
        value = pieces[0]
        for t in range(1, TYPES):
            value = jnp.where(kind == t, pieces[t], value)
        return value

    rate = by_type([coef[t] for t in range(TYPES)])
    speed = by_type([coef[TYPES + t] for t in range(TYPES)])
    main = halo[0:32]
    top = halo[32:33]
    wet = halo[35:36] > 0
    state = condense(main, top, halo[33:34], rate[0:32], rate[32:33])
    for step in range(SUB):
        gain = collect_apart(lhs, *state, turn.at[step])
        share = by_type([gain[MROWS * t : MROWS * t + MROWS] for t in range(TYPES)])
        state = (
            state[0] + (share[0:32] + share[40:72]),
            state[1] + (share[32:33] + share[72:73]),
        )
    highest = (owner & 3) == LEV - 1

    def settle(value, speed):
        above = jnp.where(highest, 0.0, pltpu.roll(value, COLS - 4, 1))
        return value + speed * (above - value)

    ghost = jnp.concatenate(
        [
            settle(jnp.where(wet, state[0], main), speed[0:32]),
            settle(jnp.broadcast_to(jnp.where(wet, state[1], top), (8, COLS)), speed[32:40]),
        ],
        axis=0,
    )

    far = jnp.broadcast_to(halo[34:35], (8, COLS))
    near = jnp.broadcast_to(edge[34:35], (8, COLS))
    lower = jnp.where(place == 0, pltpu.roll(far, 1, 1), pltpu.roll(near, 1, 1))
    upper = jnp.where(place == 3, pltpu.roll(far, COLS - 1, 1), pltpu.roll(near, COLS - 1, 1))
    left = (near + lower) * SCALE
    right = (near + upper) * SCALE
    left_abs = jnp.abs(left)
    right_abs = jnp.abs(right)

    def by_place(first, second, third, fourth):
        value = jnp.where(place == 0, first, jnp.where(place == 3, fourth, 0.0))
        return jnp.where(place == 1, second, jnp.where(place == 2, third, value))[0:1]

    own_0 = by_place(7.0 * left + 3.0 * left_abs, 0.0, 0.0, -(7.0 * right - 3.0 * right_abs))
    own_1 = by_place(-(left + left_abs), 0.0, 0.0, right - right_abs)
    halo_1 = by_place(
        (7.0 * left - 3.0 * left_abs) + (right - right_abs),
        0.0,
        0.0,
        -(7.0 * right + 3.0 * right_abs) - (left + left_abs),
    )
    halo_2 = by_place(
        left_abs - left, left_abs - left, right + right_abs, right + right_abs
    )
    inner = rim[...]
    inner_1 = jnp.where(place == 0, pltpu.roll(inner, COLS - 1, 1), pltpu.roll(inner, 1, 1))
    ghost_1 = jnp.where(place == 0, pltpu.roll(ghost, 1, 1), pltpu.roll(ghost, COLS - 1, 1))
    ghost_2 = jnp.where(place < 2, pltpu.roll(ghost, 2, 1), pltpu.roll(ghost, COLS - 2, 1))
    extra = own_0 * inner + own_1 * inner_1 + halo_1 * ghost_1 + halo_2 * ghost_2

    outer = (lane < 2) | (lane >= COLS - 2)
    pieces = [pl.ds(BINS * LEV * n, BINS * LEV) for n in range(BLK * TYPES)]
    copies = [
        pltpu.make_async_copy(final.at[rows], out.at[rows], sems.at[n])
        for n, rows in enumerate(pieces)
    ]
    for b in range(BLK):
        for t in range(TYPES):
            for l in range(LEV):
                spot = (t * BLK + b) * LEV + l
                added = jnp.where(outer, pltpu.roll(extra, (COLS - 4 * spot) % COLS, 1), 0.0)
                start = block_row(t, b) + l
                for q in range(4):
                    rows = pl.ds(start + 32 * q, 8, stride=LEV)
                    final[rows, :] = result[rows, :] + added[8 * q : 8 * q + 8]
                rows = slice(start + 128, start + 129)
                final[rows, :] = result[rows, :] + added[32:33]
            copies[b * TYPES + t].start()
    for copy in copies:
        copy.wait()


def vmem(count):
    return [pl.BlockSpec(memory_space=pltpu.VMEM)] * count


def placed(space, *arrays):
    return [pltpu.with_memory_space_constraint(x, space) for x in arrays]


def resident(*arrays):
    return placed(pltpu.VMEM, *arrays)


def body(spectra, collection, growth_rate, fall_speed, supersaturation, courant, cloudy):
    sources = (
        spectra.reshape(ROWS, COLS),
        supersaturation.reshape(BLK * LEV, COLS),
        courant.reshape(BLK * LEV, COLS),
        cloudy,
        jnp.transpose(collection, (1, 0, 2)),
        growth_rate,
        fall_speed,
    )
    edge, chosen, spec, sat, wind, wet, coll, growth, fall = pl.pallas_call(
        edge_kernel,
        out_shape=(
            pltpu.VMEM((40, COLS), F32),
            pltpu.VMEM((KDIM, KDIM), BF16),
            *(pltpu.VMEM(x.shape, x.dtype) for x in sources),
        ),
        in_specs=[pl.BlockSpec(memory_space=pltpu.HBM)] * len(sources),
        out_specs=tuple(vmem(2 + len(sources))),
        scratch_shapes=[pltpu.SemaphoreType.DMA((1 + len(sources),))],
        compiler_params=pltpu.CompilerParams(vmem_limit_bytes=LIMIT),
        name="edges",
    )(*placed(pltpu.HBM, *sources))

    def blocks(which, edge, held):
        shapes = (
            pltpu.VMEM((ROWS, COLS), F32),
            pltpu.VMEM((40, COLS), F32),
            pltpu.VMEM((TYPES * MROWS, KDIM), BF16),
            pltpu.VMEM((2 * TYPES, 40, COLS), F32),
            pltpu.VMEM((5, BLK * LEV, COLS), F32),
        )
        if which < 2:
            shapes += (pltpu.VMEM((40, COLS), F32),)
        return pl.pallas_call(
            lambda *refs: main_kernel(which, *refs),
            out_shape=shapes,
            in_specs=vmem(9 + len(held)),
            out_specs=tuple(vmem(len(shapes))),
            input_output_aliases={9 + n: n for n in range(len(held))},
            scratch_shapes=[
                pltpu.VMEM((SUB * LEV, 48, COLS), F32),
                pltpu.VMEM((KDIM // COLS, TYPES * 40, COLS), F32),
                pltpu.VMEM((TYPES * MROWS, KDIM), BF16),
                pltpu.VMEM((LEV, 40, COLS), F32),
            ],
            compiler_params=pltpu.CompilerParams(vmem_limit_bytes=LIMIT),
        )(*resident(spec, sat, wind, wet, coll, growth, fall, chosen, edge, *held))

    count = lax.axis_size("gy")
    up = [(i, (i + 1) % count) for i in range(count)]
    down = [(j, i) for i, j in up]
    *held, edge0 = blocks(0, edge, ())
    from_left = lax.ppermute(edge0, "gy", up)
    *held, edge1 = blocks(1, edge0, held)
    from_right = lax.ppermute(edge1, "gy", down)
    result, rim, lhs, coef, _ = blocks(2, edge1, held)
    out = pl.pallas_call(
        finish_kernel,
        out_shape=jax.ShapeDtypeStruct((ROWS, COLS), F32),
        in_specs=vmem(7),
        out_specs=pl.BlockSpec(memory_space=pl.ANY),
        scratch_shapes=[
            pltpu.VMEM((SUB, 48, COLS), F32),
            pltpu.VMEM((ROWS, COLS), F32),
            pltpu.SemaphoreType.DMA((BLK * TYPES,)),
        ],
        compiler_params=pltpu.CompilerParams(vmem_limit_bytes=LIMIT),
        name="finish",
    )(*resident(result, rim, from_left, from_right, edge, lhs, coef))
    return out.reshape(spectra.shape)


def solution(mesh):
    return jax.shard_map(
        body,
        mesh=mesh,
        in_specs=(
            P("gx", None, None, None, "gy"),
            P(),
            P(),
            P(),
            P("gx", None, "gy"),
            P("gx", None, "gy"),
            P("gx", "gy"),
        ),
        out_specs=P("gx", None, None, None, "gy"),
        check_vma=False,
    )
```

```python
import jax
import jax.numpy as jnp
from jax import lax
from jax.experimental import pallas as pl
from jax.experimental.pallas import tpu as pltpu
from jax.sharding import PartitionSpec as P


TYPES = 4
BINS = 33
LEV = 4
BLK = 2
SUB = 2
COLS = 128
ROWS = BLK * TYPES * BINS * LEV
PAIRS = BINS * (BINS + 1) // 2
HALF = 512
TAIL = 64
KDIM = HALF + 2 * TAIL
MROWS = 80
SCALE = 0.5 / 12.0
LIMIT = 16 << 20
F32 = jnp.float32
BF16 = jnp.bfloat16


def iota(shape, axis):
    return lax.broadcasted_iota(jnp.int32, shape, axis)


def split(x):
    high = x.astype(BF16)
    low = (x - high.astype(F32)).astype(BF16)
    return high, low


def block_row(t, b):
    return (b * TYPES + t) * BINS * LEV


def pair_of_column(col):
    tail = jnp.where(col >= HALF + TAIL, col - TAIL, col)
    first = jnp.where(col < HALF, col & 31, jnp.where(tail < 528, tail - HALF, tail - 528))
    second = jnp.where(
        col < HALF, (first + (col >> 5)) & 31, jnp.where(tail < 528, first + 16, BINS - 1)
    )
    low = jnp.minimum(first, second)
    high = jnp.maximum(first, second)
    pair = low * BINS - ((low * (low - 1)) >> 1) + (high - low)
    return jnp.where(tail > 560, -1, pair)


def edge_kernel(*refs):
    sources, edge, chosen, kept, sems = refs[:7], refs[7], refs[8], refs[9:16], refs[16]
    halves = [pl.ds(b * (ROWS // BLK), ROWS // BLK) for b in range(BLK)]
    pairs = [(sources[0].at[rows], kept[0].at[rows]) for rows in halves]
    pairs += list(zip(sources[1:], kept[1:]))
    copies = [pltpu.make_async_copy(*pair, sems.at[n]) for n, pair in enumerate(pairs)]
    for n in (2, 3, 4, 0, 1, 5, 6, 7):
        copies[n].start()
    wanted = pair_of_column(iota((1, KDIM), 1))
    for first in range(0, KDIM, COLS):
        rows = iota((COLS, KDIM), 0) + first
        chosen[first : first + COLS, :] = jnp.where(rows == wanted, 1.0, 0.0).astype(BF16)
    spec, sat, wind, cloudy = kept[:4]
    for copy in copies[2:5]:
        copy.wait()
    lane = iota((1, COLS), 1)
    owner = ((lane + 2) & 127) >> 2
    row8 = iota((8, COLS), 0)
    main = [jnp.zeros((8, COLS), F32) for _ in range(4)]
    last = jnp.zeros((8, COLS), F32)
    for b in range(BLK):
        copies[b].wait()
        cloud_row = cloudy[b : b + 1, :].astype(F32)
        for l in range(LEV):
            extra = jnp.where(
                row8 == 1,
                sat[b * LEV + l : b * LEV + l + 1, :],
                jnp.where(row8 == 2, wind[b * LEV + l : b * LEV + l + 1, :], cloud_row),
            )
            for t in range(TYPES):
                spot = (t * BLK + b) * LEV + l
                mine = owner == spot
                start = block_row(t, b) + l
                for q in range(4):
                    piece = spec[pl.ds(start + 32 * q, 8, stride=LEV), :]
                    main[q] = jnp.where(mine, pltpu.roll(piece, 4 * spot, 1), main[q])
                piece = jnp.where(row8 == 0, spec[start + 128 : start + 129, :], extra)
                last = jnp.where(mine, pltpu.roll(piece, 4 * spot, 1), last)
    for q in range(4):
        edge[8 * q : 8 * q + 8, :] = main[q]
    edge[32:40, :] = last
    for copy in copies[5:]:
        copy.wait()


def weights(left, right):
    left_abs = jnp.abs(left)
    right_abs = jnp.abs(right)
    return (
        left_abs - left,
        (right - right_abs) + (7.0 * left - 3.0 * left_abs),
        1.0 - (7.0 * right - 3.0 * right_abs) + (7.0 * left + 3.0 * left_abs),
        -(7.0 * right + 3.0 * right_abs) - (left + left_abs),
        right + right_abs,
    )


def prepare(coll, growth, fall, wind, chosen, lhs, coef, stencil, raw, parts):
    stacked = jnp.concatenate(
        [
            jnp.concatenate([growth[...], fall[...]], axis=0),
            jnp.zeros((COLS - 2 * TYPES, BINS), F32),
        ],
        axis=0,
    )
    stacked = jnp.concatenate([stacked, jnp.zeros((COLS, COLS - BINS), F32)], axis=1)
    turned = jnp.transpose(stacked)[0:40, :]
    for n in range(2 * TYPES):
        coef[n] = jnp.broadcast_to(turned[:, n : n + 1], (40, COLS))
    lane = iota((1, COLS), 1)
    own = wind[...]
    left = jnp.where(lane == 0, 0.0, (own + pltpu.roll(own, 1, 1)) * SCALE)
    right = jnp.where(lane == COLS - 1, 0.0, (own + pltpu.roll(own, COLS - 1, 1)) * SCALE)
    for by, value in zip(range(-2, 3), weights(left, right)):
        inside = (lane + by >= 0) & (lane + by < COLS)
        stencil[by + 2] = jnp.where(inside, value, 0.0)
    raw[KDIM // COLS - 1] = jnp.zeros(raw.shape[1:], F32)
    for n in range(KDIM // COLS):
        width = min(COLS, PAIRS - COLS * n)
        for k in range(BINS):
            raw[n, TYPES * k : TYPES * k + TYPES, 0:width] = coll[k, :, COLS * n : COLS * n + width]
    for t in range(TYPES):
        for n in range(KDIM // COLS):
            rows = raw[n, pl.ds(t, 40, stride=TYPES), :]
            both = jnp.concatenate(split(rows), axis=0)
            parts[MROWS * t : MROWS * t + MROWS, COLS * n : COLS * n + COLS] = both
    lhs[...] = jnp.dot(parts[...], chosen[...], preferred_element_type=F32).astype(BF16)


def condense(main, top, sat, rate_main, rate_top):
    rising = jnp.maximum(sat, 0.0)
    falling = jnp.maximum(-sat, 0.0)
    transfer = rate_main * main
    up = rising * transfer
    down = falling * transfer
    down_top = falling * (rate_top * top)
    arrive_up = jnp.concatenate([jnp.zeros_like(top), up[:-1]], axis=0)
    arrive_down = jnp.concatenate([down[1:], down_top], axis=0)
    new_main = main - up - down + arrive_up + arrive_down
    new_top = top - down_top + up[-1:]
    return new_main, new_top


def pair_parts(groups, turns):
    for (main, top), turn in zip(groups, turns):
        turn[0:32, :] = main
        turn[32:48, :] = main[0:16]

    def gather(pieces):
        return jnp.concatenate(pieces, axis=1) if len(pieces) > 1 else pieces[0]

    for first in range(0, 16, 4):
        tiles = []
        for (main, _), turn in zip(groups, turns):
            parts = [
                split(main * (main if d == 0 else turn[d : d + 32, :]))
                for d in range(first, first + 4)
            ]
            tiles.append(jnp.concatenate([p[0] for p in parts] + [p[1] for p in parts], axis=0))
        columns = slice(32 * first, 32 * first + 128)
        yield (columns, columns), gather(tiles)
    tails = []
    for main, top in groups:
        square = jnp.where(iota((16, COLS), 0) == 0, top * top, 0.0)
        rest = jnp.concatenate([main[0:16] * main[16:32], main * top, square], axis=0)
        tails.append(jnp.concatenate(split(rest), axis=0))
    yield (slice(HALF, KDIM),), gather(tails)


def collect(lhs, groups, turns):
    total = None
    for columns, part in pair_parts(groups, turns):
        gain = jnp.dot(
            jnp.concatenate([lhs[:, c] for c in columns], axis=1), part, preferred_element_type=F32
        )
        total = gain if total is None else total + gain
    return total


def collect_apart(lhs, main, top, turn):
    turn[0:32, :] = main
    turn[32:48, :] = main[0:16]
    total = None
    for first in range(0, 16, 8):
        value = jnp.concatenate(
            [main * (main if d == 0 else turn[d : d + 32, :]) for d in range(first, first + 8)],
            axis=0,
        )
        part = jnp.concatenate(split(value), axis=1)
        gain = jnp.dot(lhs[:, 32 * first : 32 * first + 256], part, preferred_element_type=F32)
        total = gain if total is None else total + gain
    square = jnp.where(iota((16, COLS), 0) == 0, top * top, 0.0)
    rest = jnp.concatenate([main[0:16] * main[16:32], main * top, square], axis=0)
    part = jnp.concatenate(split(rest), axis=1)
    total = total + jnp.dot(lhs[:, HALF : HALF + TAIL], part, preferred_element_type=F32)
    return total[:, 0:COLS] + total[:, COLS : 2 * COLS]


UP = ((6, 4, 3, 1, 0, 0, 0, 0), (6, 5, 4, 2, 1, 1, 1, 0))
DOWN = ((7, 5, 4, 2, 1, 1, 1, 0), (6, 5, 4, 2, 1, 1, 1, 0))


def shares():
    x, y = lax.axis_index("gx"), lax.axis_index("gy")

    def pick(table):
        value = jnp.int32(0)
        for odd in range(2):
            for z, count in enumerate(table[odd]):
                value = jnp.where(y == 2 * z + odd, count, value)
        return value

    first, second = pick(UP), pick(DOWN)
    for n, pair in enumerate(((0, 1), (6, 6), (1, 2), (4, 5))):
        special = (x == 0) & (y == n)
        first = jnp.where(special, pair[0], first)
        second = jnp.where(special, pair[1], second)
    return (0, first), (first, second), (second, BLK * TYPES)


def main_kernel(which, spec, sat, wind, cloudy, coll, growth, fall, chosen, edge, *rest):
    result, rim, lhs, coef, stencil = rest[-10:-5] if which < 2 else rest[-9:-4]
    turn, raw, parts, held = rest[-4:]
    if which < 2:
        rest[-5][...] = edge[...]
    begin, end = shares()[which]
    owner = ((iota((1, COLS), 1) + 2) & (COLS - 1)) >> 2

    @pl.when((begin == 0) & (end > 0))
    def _():
        prepare(coll, growth, fall, wind, chosen, lhs, coef, stencil, raw, parts)

    def advect(n):
        t = n >> 1
        b = n & 1
        start = block_row(t, b)
        for l in range(LEV):
            settled = held[l]
            spot = n * LEV + l
            rim[...] = jnp.where(owner == spot, pltpu.roll(settled, 4 * spot, 1), rim[...])
            w = [stencil[k, pl.ds(b * LEV + l, 1), :] for k in range(5)]
            y = w[2] * settled
            for by in (-2, -1, 1, 2):
                y = y + w[by + 2] * pltpu.roll(settled, (COLS - by) % COLS, 1)
            for q in range(4):
                result[pl.ds(start + l + 32 * q, 8, stride=LEV), :] = y[8 * q : 8 * q + 8]
            result[pl.ds(start + l + 128, 1), :] = y[32:33]

    def one(n, carry):
        advect(jnp.maximum(n - 1, begin))
        t = n >> 1
        b = n & 1
        start = block_row(t, b)
        left = lhs[pl.ds(pl.multiple_of(t * MROWS, 16), MROWS), :]
        rate = coef[t]
        speed = coef[TYPES + t]
        wet = cloudy[pl.ds(b, 1), :] > 0
        before = []
        state = []
        for l in range(LEV):
            main = spec[pl.ds(start + l, 32, stride=LEV), :]
            top = spec[pl.ds(start + 128 + l, 1), :]
            before.append((main, top))
            row = sat[pl.ds(b * LEV + l, 1), :]
            state.append(condense(main, top, row, rate[0:32], rate[32:33]))
        for step in range(SUB):
            for half in range(2):
                levels = range(2 * half, 2 * half + 2)
                gain = collect(
                    left,
                    [state[l] for l in levels],
                    [turn.at[LEV * step + l] for l in levels],
                )
                for k in range(2):
                    l = 2 * half + k
                    mine = gain[:, COLS * k : COLS * k + COLS]
                    main, top = state[l]
                    state[l] = (
                        main + (mine[0:32] + mine[40:72]),
                        top + (mine[32:33] + mine[72:73]),
                    )
        above = None
        for l in reversed(range(LEV)):
            main = jnp.where(wet, state[l][0], before[l][0])
            top = jnp.where(wet, state[l][1], before[l][1])
            over = (jnp.zeros_like(main), jnp.zeros_like(top)) if above is None else above
            held[l, 0:32, :] = main + speed[0:32] * (over[0] - main)
            held[l, 32:40, :] = jnp.broadcast_to(top + speed[32:33] * (over[1] - top), (8, COLS))
            above = (main, top)
        return carry

    lax.fori_loop(begin, end, one, 0)

    @pl.when(end > begin)
    def _():
        advect(end - 1)


def finish_kernel(result, rim, from_left, from_right, edge, lhs, coef, out, turn, final, sems):
    lane = iota((1, COLS), 1)
    owner = ((lane + 2) & 127) >> 2
    kind = owner >> 3
    place = lane & 3
    halo = jnp.where(place < 2, from_right[...], from_left[...])

    def by_type(pieces):
        value = pieces[0]
        for t in range(1, TYPES):
            value = jnp.where(kind == t, pieces[t], value)
        return value

    rate = by_type([coef[t] for t in range(TYPES)])
    speed = by_type([coef[TYPES + t] for t in range(TYPES)])
    main = halo[0:32]
    top = halo[32:33]
    wet = halo[35:36] > 0
    state = condense(main, top, halo[33:34], rate[0:32], rate[32:33])
    for step in range(SUB):
        gain = collect_apart(lhs, *state, turn.at[step])
        share = by_type([gain[MROWS * t : MROWS * t + MROWS] for t in range(TYPES)])
        state = (
            state[0] + (share[0:32] + share[40:72]),
            state[1] + (share[32:33] + share[72:73]),
        )
    highest = (owner & 3) == LEV - 1

    def settle(value, speed):
        above = jnp.where(highest, 0.0, pltpu.roll(value, COLS - 4, 1))
        return value + speed * (above - value)

    ghost = jnp.concatenate(
        [
            settle(jnp.where(wet, state[0], main), speed[0:32]),
            settle(jnp.broadcast_to(jnp.where(wet, state[1], top), (8, COLS)), speed[32:40]),
        ],
        axis=0,
    )

    far = jnp.broadcast_to(halo[34:35], (8, COLS))
    near = jnp.broadcast_to(edge[34:35], (8, COLS))
    lower = jnp.where(place == 0, pltpu.roll(far, 1, 1), pltpu.roll(near, 1, 1))
    upper = jnp.where(place == 3, pltpu.roll(far, COLS - 1, 1), pltpu.roll(near, COLS - 1, 1))
    left = (near + lower) * SCALE
    right = (near + upper) * SCALE
    left_abs = jnp.abs(left)
    right_abs = jnp.abs(right)

    def by_place(first, second, third, fourth):
        value = jnp.where(place == 0, first, jnp.where(place == 3, fourth, 0.0))
        return jnp.where(place == 1, second, jnp.where(place == 2, third, value))[0:1]

    own_0 = by_place(7.0 * left + 3.0 * left_abs, 0.0, 0.0, -(7.0 * right - 3.0 * right_abs))
    own_1 = by_place(-(left + left_abs), 0.0, 0.0, right - right_abs)
    halo_1 = by_place(
        (7.0 * left - 3.0 * left_abs) + (right - right_abs),
        0.0,
        0.0,
        -(7.0 * right + 3.0 * right_abs) - (left + left_abs),
    )
    halo_2 = by_place(
        left_abs - left, left_abs - left, right + right_abs, right + right_abs
    )
    inner = rim[...]
    inner_1 = jnp.where(place == 0, pltpu.roll(inner, COLS - 1, 1), pltpu.roll(inner, 1, 1))
    ghost_1 = jnp.where(place == 0, pltpu.roll(ghost, 1, 1), pltpu.roll(ghost, COLS - 1, 1))
    ghost_2 = jnp.where(place < 2, pltpu.roll(ghost, 2, 1), pltpu.roll(ghost, COLS - 2, 1))
    extra = own_0 * inner + own_1 * inner_1 + halo_1 * ghost_1 + halo_2 * ghost_2

    outer = (lane < 2) | (lane >= COLS - 2)
    pieces = [pl.ds(2 * BINS * LEV * n, 2 * BINS * LEV) for n in range(BLK * TYPES // 2)]
    copies = [
        pltpu.make_async_copy(final.at[rows], out.at[rows], sems.at[n])
        for n, rows in enumerate(pieces)
    ]
    for b in range(BLK):
        for t in range(TYPES):
            for l in range(LEV):
                spot = (t * BLK + b) * LEV + l
                added = jnp.where(outer, pltpu.roll(extra, (COLS - 4 * spot) % COLS, 1), 0.0)
                start = block_row(t, b) + l
                for q in range(4):
                    rows = pl.ds(start + 32 * q, 8, stride=LEV)
                    final[rows, :] = result[rows, :] + added[8 * q : 8 * q + 8]
                rows = slice(start + 128, start + 129)
                final[rows, :] = result[rows, :] + added[32:33]
            if t & 1:
                copies[(b * TYPES + t) // 2].start()
    for copy in copies:
        copy.wait()


def vmem(count):
    return [pl.BlockSpec(memory_space=pltpu.VMEM)] * count


def placed(space, *arrays):
    return [pltpu.with_memory_space_constraint(x, space) for x in arrays]


def resident(*arrays):
    return placed(pltpu.VMEM, *arrays)


def body(spectra, collection, growth_rate, fall_speed, supersaturation, courant, cloudy):
    sources = (
        spectra.reshape(ROWS, COLS),
        supersaturation.reshape(BLK * LEV, COLS),
        courant.reshape(BLK * LEV, COLS),
        cloudy,
        jnp.transpose(collection, (1, 0, 2)),
        growth_rate,
        fall_speed,
    )
    edge, chosen, spec, sat, wind, wet, coll, growth, fall = pl.pallas_call(
        edge_kernel,
        out_shape=(
            pltpu.VMEM((40, COLS), F32),
            pltpu.VMEM((KDIM, KDIM), BF16),
            *(pltpu.VMEM(x.shape, x.dtype) for x in sources),
        ),
        in_specs=[pl.BlockSpec(memory_space=pltpu.HBM)] * len(sources),
        out_specs=tuple(vmem(2 + len(sources))),
        scratch_shapes=[pltpu.SemaphoreType.DMA((1 + len(sources),))],
        compiler_params=pltpu.CompilerParams(vmem_limit_bytes=LIMIT),
        name="edges",
    )(*placed(pltpu.HBM, *sources))

    def blocks(which, edge, held):
        shapes = (
            pltpu.VMEM((ROWS, COLS), F32),
            pltpu.VMEM((40, COLS), F32),
            pltpu.VMEM((TYPES * MROWS, KDIM), BF16),
            pltpu.VMEM((2 * TYPES, 40, COLS), F32),
            pltpu.VMEM((5, BLK * LEV, COLS), F32),
        )
        if which < 2:
            shapes += (pltpu.VMEM((40, COLS), F32),)
        return pl.pallas_call(
            lambda *refs: main_kernel(which, *refs),
            out_shape=shapes,
            in_specs=vmem(9 + len(held)),
            out_specs=tuple(vmem(len(shapes))),
            input_output_aliases={9 + n: n for n in range(len(held))},
            scratch_shapes=[
                pltpu.VMEM((SUB * LEV, 48, COLS), F32),
                pltpu.VMEM((KDIM // COLS, TYPES * 40, COLS), F32),
                pltpu.VMEM((TYPES * MROWS, KDIM), BF16),
                pltpu.VMEM((LEV, 40, COLS), F32),
            ],
            compiler_params=pltpu.CompilerParams(vmem_limit_bytes=LIMIT),
        )(*resident(spec, sat, wind, wet, coll, growth, fall, chosen, edge, *held))

    count = lax.axis_size("gy")
    up = [(i, (i + 1) % count) for i in range(count)]
    down = [(j, i) for i, j in up]
    *held, edge0 = blocks(0, edge, ())
    from_left = lax.ppermute(edge0, "gy", up)
    *held, edge1 = blocks(1, edge0, held)
    from_right = lax.ppermute(edge1, "gy", down)
    result, rim, lhs, coef, _ = blocks(2, edge1, held)
    out = pl.pallas_call(
        finish_kernel,
        out_shape=jax.ShapeDtypeStruct((ROWS, COLS), F32),
        in_specs=vmem(7),
        out_specs=pl.BlockSpec(memory_space=pl.ANY),
        scratch_shapes=[
            pltpu.VMEM((SUB, 48, COLS), F32),
            pltpu.VMEM((ROWS, COLS), F32),
            pltpu.SemaphoreType.DMA((BLK * TYPES // 2,)),
        ],
        compiler_params=pltpu.CompilerParams(vmem_limit_bytes=LIMIT),
        name="finish",
    )(*resident(result, rim, from_left, from_right, edge, lhs, coef))
    return out.reshape(spectra.shape)


def solution(mesh):
    return jax.shard_map(
        body,
        mesh=mesh,
        in_specs=(
            P("gx", None, None, None, "gy"),
            P(),
            P(),
            P(),
            P("gx", None, "gy"),
            P("gx", None, "gy"),
            P("gx", "gy"),
        ),
        out_specs=P("gx", None, None, None, "gy"),
        check_vma=False,
    )
```

```python
import jax
import jax.numpy as jnp
from jax import lax
from jax.experimental import pallas as pl
from jax.experimental.pallas import tpu as pltpu
from jax.sharding import PartitionSpec as P


TYPES = 4
BINS = 33
LEV = 4
BLK = 2
SUB = 2
COLS = 128
ROWS = BLK * TYPES * BINS * LEV
PAIRS = BINS * (BINS + 1) // 2
HALF = 512
TAIL = 64
KDIM = HALF + 2 * TAIL
MROWS = 80
SCALE = 0.5 / 12.0
LIMIT = 16 << 20
F32 = jnp.float32
BF16 = jnp.bfloat16


def iota(shape, axis):
    return lax.broadcasted_iota(jnp.int32, shape, axis)


def split(x):
    high = x.astype(BF16)
    low = (x - high.astype(F32)).astype(BF16)
    return high, low


def block_row(t, b):
    return (b * TYPES + t) * BINS * LEV


def pair_of_column(col):
    tail = jnp.where(col >= HALF + TAIL, col - TAIL, col)
    first = jnp.where(col < HALF, col & 31, jnp.where(tail < 528, tail - HALF, tail - 528))
    second = jnp.where(
        col < HALF, (first + (col >> 5)) & 31, jnp.where(tail < 528, first + 16, BINS - 1)
    )
    low = jnp.minimum(first, second)
    high = jnp.maximum(first, second)
    pair = low * BINS - ((low * (low - 1)) >> 1) + (high - low)
    return jnp.where(tail > 560, -1, pair)


def edge_kernel(*refs):
    sources, edge, chosen, kept, sems = refs[:7], refs[7], refs[8], refs[9:16], refs[16]
    halves = [pl.ds(b * (ROWS // BLK), ROWS // BLK) for b in range(BLK)]
    pairs = [(sources[0].at[rows], kept[0].at[rows]) for rows in halves]
    pairs += list(zip(sources[1:], kept[1:]))
    copies = [pltpu.make_async_copy(*pair, sems.at[n]) for n, pair in enumerate(pairs)]
    for n in (2, 3, 4, 0, 1, 5, 6, 7):
        copies[n].start()
    wanted = pair_of_column(iota((1, KDIM), 1))
    for first in range(0, KDIM, COLS):
        rows = iota((COLS, KDIM), 0) + first
        chosen[first : first + COLS, :] = jnp.where(rows == wanted, 1.0, 0.0).astype(BF16)
    spec, sat, wind, cloudy = kept[:4]
    for copy in copies[2:5]:
        copy.wait()
    lane = iota((1, COLS), 1)
    owner = ((lane + 2) & 127) >> 2
    row8 = iota((8, COLS), 0)
    main = [jnp.zeros((8, COLS), F32) for _ in range(4)]
    last = jnp.zeros((8, COLS), F32)
    for b in range(BLK):
        copies[b].wait()
        cloud_row = cloudy[b : b + 1, :].astype(F32)
        for l in range(LEV):
            extra = jnp.where(
                row8 == 1,
                sat[b * LEV + l : b * LEV + l + 1, :],
                jnp.where(row8 == 2, wind[b * LEV + l : b * LEV + l + 1, :], cloud_row),
            )
            for t in range(TYPES):
                spot = (t * BLK + b) * LEV + l
                mine = owner == spot
                start = block_row(t, b) + l
                for q in range(4):
                    piece = spec[pl.ds(start + 32 * q, 8, stride=LEV), :]
                    main[q] = jnp.where(mine, pltpu.roll(piece, 4 * spot, 1), main[q])
                piece = jnp.where(row8 == 0, spec[start + 128 : start + 129, :], extra)
                last = jnp.where(mine, pltpu.roll(piece, 4 * spot, 1), last)
    for q in range(4):
        edge[8 * q : 8 * q + 8, :] = main[q]
    edge[32:40, :] = last
    for copy in copies[5:]:
        copy.wait()


def weights(left, right):
    left_abs = jnp.abs(left)
    right_abs = jnp.abs(right)
    return (
        left_abs - left,
        (right - right_abs) + (7.0 * left - 3.0 * left_abs),
        1.0 - (7.0 * right - 3.0 * right_abs) + (7.0 * left + 3.0 * left_abs),
        -(7.0 * right + 3.0 * right_abs) - (left + left_abs),
        right + right_abs,
    )


def prepare(coll, growth, fall, wind, chosen, lhs, coef, stencil, raw, parts):
    stacked = jnp.concatenate(
        [
            jnp.concatenate([growth[...], fall[...]], axis=0),
            jnp.zeros((COLS - 2 * TYPES, BINS), F32),
        ],
        axis=0,
    )
    stacked = jnp.concatenate([stacked, jnp.zeros((COLS, COLS - BINS), F32)], axis=1)
    turned = jnp.transpose(stacked)[0:40, :]
    for n in range(2 * TYPES):
        coef[n] = jnp.broadcast_to(turned[:, n : n + 1], (40, COLS))
    lane = iota((1, COLS), 1)
    own = wind[...]
    left = jnp.where(lane == 0, 0.0, (own + pltpu.roll(own, 1, 1)) * SCALE)
    right = jnp.where(lane == COLS - 1, 0.0, (own + pltpu.roll(own, COLS - 1, 1)) * SCALE)
    for by, value in zip(range(-2, 3), weights(left, right)):
        inside = (lane + by >= 0) & (lane + by < COLS)
        stencil[by + 2] = jnp.where(inside, value, 0.0)
    raw[KDIM // COLS - 1] = jnp.zeros(raw.shape[1:], F32)
    for n in range(KDIM // COLS):
        width = min(COLS, PAIRS - COLS * n)
        for k in range(BINS):
            raw[n, TYPES * k : TYPES * k + TYPES, 0:width] = coll[k, :, COLS * n : COLS * n + width]
    for t in range(TYPES):
        for n in range(KDIM // COLS):
            rows = raw[n, pl.ds(t, 40, stride=TYPES), :]
            both = jnp.concatenate(split(rows), axis=0)
            parts[MROWS * t : MROWS * t + MROWS, COLS * n : COLS * n + COLS] = both
    lhs[...] = jnp.dot(parts[...], chosen[...], preferred_element_type=F32).astype(BF16)


def condense(main, top, sat, rate_main, rate_top):
    rising = jnp.maximum(sat, 0.0)
    falling = jnp.maximum(-sat, 0.0)
    transfer = rate_main * main
    up = rising * transfer
    down = falling * transfer
    down_top = falling * (rate_top * top)
    arrive_up = jnp.concatenate([jnp.zeros_like(top), up[:-1]], axis=0)
    arrive_down = jnp.concatenate([down[1:], down_top], axis=0)
    new_main = main - up - down + arrive_up + arrive_down
    new_top = top - down_top + up[-1:]
    return new_main, new_top


def pair_parts(groups, turns):
    for (main, top), turn in zip(groups, turns):
        turn[0:32, :] = main
        turn[32:48, :] = main[0:16]

    def gather(pieces):
        return jnp.concatenate(pieces, axis=1) if len(pieces) > 1 else pieces[0]

    for first in range(0, 16, 4):
        tiles = []
        for (main, _), turn in zip(groups, turns):
            parts = [
                split(main * (main if d == 0 else turn[d : d + 32, :]))
                for d in range(first, first + 4)
            ]
            tiles.append(jnp.concatenate([p[0] for p in parts] + [p[1] for p in parts], axis=0))
        columns = slice(32 * first, 32 * first + 128)
        yield (columns, columns), gather(tiles)
    tails = []
    for main, top in groups:
        square = jnp.where(iota((16, COLS), 0) == 0, top * top, 0.0)
        rest = jnp.concatenate([main[0:16] * main[16:32], main * top, square], axis=0)
        tails.append(jnp.concatenate(split(rest), axis=0))
    yield (slice(HALF, KDIM),), gather(tails)


def collect(lhs, groups, turns):
    total = None
    for columns, part in pair_parts(groups, turns):
        gain = jnp.dot(
            jnp.concatenate([lhs[:, c] for c in columns], axis=1), part, preferred_element_type=F32
        )
        total = gain if total is None else total + gain
    return total


def collect_apart(lhs, main, top, turn):
    turn[0:32, :] = main
    turn[32:48, :] = main[0:16]
    total = None
    for first in range(0, 16, 8):
        value = jnp.concatenate(
            [main * (main if d == 0 else turn[d : d + 32, :]) for d in range(first, first + 8)],
            axis=0,
        )
        part = jnp.concatenate(split(value), axis=1)
        gain = jnp.dot(lhs[:, 32 * first : 32 * first + 256], part, preferred_element_type=F32)
        total = gain if total is None else total + gain
    square = jnp.where(iota((16, COLS), 0) == 0, top * top, 0.0)
    rest = jnp.concatenate([main[0:16] * main[16:32], main * top, square], axis=0)
    part = jnp.concatenate(split(rest), axis=1)
    total = total + jnp.dot(lhs[:, HALF : HALF + TAIL], part, preferred_element_type=F32)
    return total[:, 0:COLS] + total[:, COLS : 2 * COLS]


UP = ((6, 4, 3, 1, 0, 0, 0, 0), (6, 5, 4, 2, 1, 1, 1, 0))
DOWN = ((7, 5, 4, 2, 1, 1, 1, 0), (6, 5, 4, 2, 1, 1, 1, 0))


def shares():
    x, y = lax.axis_index("gx"), lax.axis_index("gy")

    def pick(table):
        value = jnp.int32(0)
        for odd in range(2):
            for z, count in enumerate(table[odd]):
                value = jnp.where(y == 2 * z + odd, count, value)
        return value

    first, second = pick(UP), pick(DOWN)
    for n, pair in enumerate(((0, 1), (6, 6), (1, 2), (4, 5))):
        special = (x == 0) & (y == n)
        first = jnp.where(special, pair[0], first)
        second = jnp.where(special, pair[1], second)
    return (0, first), (first, second), (second, BLK * TYPES)


def main_kernel(which, spec, sat, wind, cloudy, coll, growth, fall, chosen, edge, *rest):
    result, rim, lhs, coef, stencil = rest[-10:-5] if which < 2 else rest[-9:-4]
    turn, raw, parts, held = rest[-4:]
    if which < 2:
        rest[-5][...] = edge[...]
    begin, end = shares()[which]
    owner = ((iota((1, COLS), 1) + 2) & (COLS - 1)) >> 2

    @pl.when((begin == 0) & (end > 0))
    def _():
        prepare(coll, growth, fall, wind, chosen, lhs, coef, stencil, raw, parts)

    def advect(n):
        t = n >> 1
        b = n & 1
        start = block_row(t, b)
        for l in range(LEV):
            settled = held[l]
            spot = n * LEV + l
            rim[...] = jnp.where(owner == spot, pltpu.roll(settled, 4 * spot, 1), rim[...])
            w = [stencil[k, pl.ds(b * LEV + l, 1), :] for k in range(5)]
            y = w[2] * settled
            for by in (-2, -1, 1, 2):
                y = y + w[by + 2] * pltpu.roll(settled, (COLS - by) % COLS, 1)
            for q in range(4):
                result[pl.ds(start + l + 32 * q, 8, stride=LEV), :] = y[8 * q : 8 * q + 8]
            result[pl.ds(start + l + 128, 1), :] = y[32:33]

    def one(n, carry):
        advect(jnp.maximum(n - 1, begin))
        t = n >> 1
        b = n & 1
        start = block_row(t, b)
        left = lhs[pl.ds(pl.multiple_of(t * MROWS, 16), MROWS), :]
        rate = coef[t]
        speed = coef[TYPES + t]
        wet = cloudy[pl.ds(b, 1), :] > 0
        before = []
        state = []
        for l in range(LEV):
            main = spec[pl.ds(start + l, 32, stride=LEV), :]
            top = spec[pl.ds(start + 128 + l, 1), :]
            before.append((main, top))
            row = sat[pl.ds(b * LEV + l, 1), :]
            state.append(condense(main, top, row, rate[0:32], rate[32:33]))
        for step in range(SUB):
            for half in range(2):
                levels = range(2 * half, 2 * half + 2)
                gain = collect(
                    left,
                    [state[l] for l in levels],
                    [turn.at[LEV * step + l] for l in levels],
                )
                for k in range(2):
                    l = 2 * half + k
                    mine = gain[:, COLS * k : COLS * k + COLS]
                    main, top = state[l]
                    state[l] = (
                        main + (mine[0:32] + mine[40:72]),
                        top + (mine[32:33] + mine[72:73]),
                    )
        above = None
        for l in reversed(range(LEV)):
            main = jnp.where(wet, state[l][0], before[l][0])
            top = jnp.where(wet, state[l][1], before[l][1])
            over = (jnp.zeros_like(main), jnp.zeros_like(top)) if above is None else above
            held[l, 0:32, :] = main + speed[0:32] * (over[0] - main)
            held[l, 32:40, :] = jnp.broadcast_to(top + speed[32:33] * (over[1] - top), (8, COLS))
            above = (main, top)
        return carry

    lax.fori_loop(begin, end, one, 0)

    @pl.when(end > begin)
    def _():
        advect(end - 1)


def finish_kernel(result, rim, from_left, from_right, edge, lhs, coef, out, turn, final, sems):
    lane = iota((1, COLS), 1)
    owner = ((lane + 2) & 127) >> 2
    kind = owner >> 3
    place = lane & 3
    halo = jnp.where(place < 2, from_right[...], from_left[...])

    def by_type(pieces):
        value = pieces[0]
        for t in range(1, TYPES):
            value = jnp.where(kind == t, pieces[t], value)
        return value

    rate = by_type([coef[t] for t in range(TYPES)])
    speed = by_type([coef[TYPES + t] for t in range(TYPES)])
    main = halo[0:32]
    top = halo[32:33]
    wet = halo[35:36] > 0
    state = condense(main, top, halo[33:34], rate[0:32], rate[32:33])
    for step in range(SUB):
        gain = collect_apart(lhs, *state, turn.at[step])
        share = by_type([gain[MROWS * t : MROWS * t + MROWS] for t in range(TYPES)])
        state = (
            state[0] + (share[0:32] + share[40:72]),
            state[1] + (share[32:33] + share[72:73]),
        )
    highest = (owner & 3) == LEV - 1

    def settle(value, speed):
        above = jnp.where(highest, 0.0, pltpu.roll(value, COLS - 4, 1))
        return value + speed * (above - value)

    ghost = jnp.concatenate(
        [
            settle(jnp.where(wet, state[0], main), speed[0:32]),
            settle(jnp.broadcast_to(jnp.where(wet, state[1], top), (8, COLS)), speed[32:40]),
        ],
        axis=0,
    )

    far = jnp.broadcast_to(halo[34:35], (8, COLS))
    near = jnp.broadcast_to(edge[34:35], (8, COLS))
    lower = jnp.where(place == 0, pltpu.roll(far, 1, 1), pltpu.roll(near, 1, 1))
    upper = jnp.where(place == 3, pltpu.roll(far, COLS - 1, 1), pltpu.roll(near, COLS - 1, 1))
    left = (near + lower) * SCALE
    right = (near + upper) * SCALE
    left_abs = jnp.abs(left)
    right_abs = jnp.abs(right)

    def by_place(first, second, third, fourth):
        value = jnp.where(place == 0, first, jnp.where(place == 3, fourth, 0.0))
        return jnp.where(place == 1, second, jnp.where(place == 2, third, value))[0:1]

    own_0 = by_place(7.0 * left + 3.0 * left_abs, 0.0, 0.0, -(7.0 * right - 3.0 * right_abs))
    own_1 = by_place(-(left + left_abs), 0.0, 0.0, right - right_abs)
    halo_1 = by_place(
        (7.0 * left - 3.0 * left_abs) + (right - right_abs),
        0.0,
        0.0,
        -(7.0 * right + 3.0 * right_abs) - (left + left_abs),
    )
    halo_2 = by_place(
        left_abs - left, left_abs - left, right + right_abs, right + right_abs
    )
    inner = rim[...]
    inner_1 = jnp.where(place == 0, pltpu.roll(inner, COLS - 1, 1), pltpu.roll(inner, 1, 1))
    ghost_1 = jnp.where(place == 0, pltpu.roll(ghost, 1, 1), pltpu.roll(ghost, COLS - 1, 1))
    ghost_2 = jnp.where(place < 2, pltpu.roll(ghost, 2, 1), pltpu.roll(ghost, COLS - 2, 1))
    extra = own_0 * inner + own_1 * inner_1 + halo_1 * ghost_1 + halo_2 * ghost_2

    outer = (lane < 2) | (lane >= COLS - 2)
    bounds = [BINS * LEV * n // 8 * 8 for n in range(BLK * TYPES + 1)]
    pieces = [pl.ds(low, high - low) for low, high in zip(bounds, bounds[1:])]
    copies = [
        pltpu.make_async_copy(final.at[rows], out.at[rows], sems.at[n])
        for n, rows in enumerate(pieces)
    ]
    for b in range(BLK):
        for t in range(TYPES):
            for l in range(LEV):
                spot = (t * BLK + b) * LEV + l
                added = jnp.where(outer, pltpu.roll(extra, (COLS - 4 * spot) % COLS, 1), 0.0)
                start = block_row(t, b) + l
                for q in range(4):
                    rows = pl.ds(start + 32 * q, 8, stride=LEV)
                    final[rows, :] = result[rows, :] + added[8 * q : 8 * q + 8]
                rows = slice(start + 128, start + 129)
                final[rows, :] = result[rows, :] + added[32:33]
            copies[b * TYPES + t].start()
    for copy in copies:
        copy.wait()


def vmem(count):
    return [pl.BlockSpec(memory_space=pltpu.VMEM)] * count


def placed(space, *arrays):
    return [pltpu.with_memory_space_constraint(x, space) for x in arrays]


def resident(*arrays):
    return placed(pltpu.VMEM, *arrays)


def body(spectra, collection, growth_rate, fall_speed, supersaturation, courant, cloudy):
    sources = (
        spectra.reshape(ROWS, COLS),
        supersaturation.reshape(BLK * LEV, COLS),
        courant.reshape(BLK * LEV, COLS),
        cloudy,
        jnp.transpose(collection, (1, 0, 2)),
        growth_rate,
        fall_speed,
    )
    edge, chosen, spec, sat, wind, wet, coll, growth, fall = pl.pallas_call(
        edge_kernel,
        out_shape=(
            pltpu.VMEM((40, COLS), F32),
            pltpu.VMEM((KDIM, KDIM), BF16),
            *(pltpu.VMEM(x.shape, x.dtype) for x in sources),
        ),
        in_specs=[pl.BlockSpec(memory_space=pltpu.HBM)] * len(sources),
        out_specs=tuple(vmem(2 + len(sources))),
        scratch_shapes=[pltpu.SemaphoreType.DMA((1 + len(sources),))],
        compiler_params=pltpu.CompilerParams(vmem_limit_bytes=LIMIT),
        name="edges",
    )(*placed(pltpu.HBM, *sources))

    def blocks(which, edge, held):
        shapes = (
            pltpu.VMEM((ROWS, COLS), F32),
            pltpu.VMEM((40, COLS), F32),
            pltpu.VMEM((TYPES * MROWS, KDIM), BF16),
            pltpu.VMEM((2 * TYPES, 40, COLS), F32),
            pltpu.VMEM((5, BLK * LEV, COLS), F32),
        )
        if which < 2:
            shapes += (pltpu.VMEM((40, COLS), F32),)
        return pl.pallas_call(
            lambda *refs: main_kernel(which, *refs),
            out_shape=shapes,
            in_specs=vmem(9 + len(held)),
            out_specs=tuple(vmem(len(shapes))),
            input_output_aliases={9 + n: n for n in range(len(held))},
            scratch_shapes=[
                pltpu.VMEM((SUB * LEV, 48, COLS), F32),
                pltpu.VMEM((KDIM // COLS, TYPES * 40, COLS), F32),
                pltpu.VMEM((TYPES * MROWS, KDIM), BF16),
                pltpu.VMEM((LEV, 40, COLS), F32),
            ],
            compiler_params=pltpu.CompilerParams(vmem_limit_bytes=LIMIT),
        )(*resident(spec, sat, wind, wet, coll, growth, fall, chosen, edge, *held))

    count = lax.axis_size("gy")
    up = [(i, (i + 1) % count) for i in range(count)]
    down = [(j, i) for i, j in up]
    *held, edge0 = blocks(0, edge, ())
    from_left = lax.ppermute(edge0, "gy", up)
    *held, edge1 = blocks(1, edge0, held)
    from_right = lax.ppermute(edge1, "gy", down)
    result, rim, lhs, coef, _ = blocks(2, edge1, held)
    out = pl.pallas_call(
        finish_kernel,
        out_shape=jax.ShapeDtypeStruct((ROWS, COLS), F32),
        in_specs=vmem(7),
        out_specs=pl.BlockSpec(memory_space=pl.ANY),
        scratch_shapes=[
            pltpu.VMEM((SUB, 48, COLS), F32),
            pltpu.VMEM((ROWS, COLS), F32),
            pltpu.SemaphoreType.DMA((BLK * TYPES,)),
        ],
        compiler_params=pltpu.CompilerParams(vmem_limit_bytes=LIMIT),
        name="finish",
    )(*resident(result, rim, from_left, from_right, edge, lhs, coef))
    return out.reshape(spectra.shape)


def solution(mesh):
    return jax.shard_map(
        body,
        mesh=mesh,
        in_specs=(
            P("gx", None, None, None, "gy"),
            P(),
            P(),
            P(),
            P("gx", None, "gy"),
            P("gx", None, "gy"),
            P("gx", "gy"),
        ),
        out_specs=P("gx", None, None, None, "gy"),
        check_vma=False,
    )
```

```python
import jax
import jax.numpy as jnp
from jax import lax
from jax.experimental import pallas as pl
from jax.experimental.pallas import tpu as pltpu
from jax.sharding import PartitionSpec as P


TYPES = 4
BINS = 33
LEV = 4
BLK = 2
SUB = 2
COLS = 128
ROWS = BLK * TYPES * BINS * LEV
PAIRS = BINS * (BINS + 1) // 2
HALF = 512
TAIL = 64
KDIM = HALF + 2 * TAIL
MROWS = 80
SCALE = 0.5 / 12.0
LIMIT = 16 << 20
F32 = jnp.float32
BF16 = jnp.bfloat16


def iota(shape, axis):
    return lax.broadcasted_iota(jnp.int32, shape, axis)


def split(x):
    high = x.astype(BF16)
    low = (x - high.astype(F32)).astype(BF16)
    return high, low


def block_row(t, b):
    return (b * TYPES + t) * BINS * LEV


def pair_of_column(col):
    tail = jnp.where(col >= HALF + TAIL, col - TAIL, col)
    first = jnp.where(col < HALF, col & 31, jnp.where(tail < 528, tail - HALF, tail - 528))
    second = jnp.where(
        col < HALF, (first + (col >> 5)) & 31, jnp.where(tail < 528, first + 16, BINS - 1)
    )
    low = jnp.minimum(first, second)
    high = jnp.maximum(first, second)
    pair = low * BINS - ((low * (low - 1)) >> 1) + (high - low)
    return jnp.where(tail > 560, -1, pair)


def edge_kernel(*refs):
    sources, edge, chosen, kept, sems = refs[:7], refs[7], refs[8], refs[9:16], refs[16]
    pieces = [pl.ds(2 * BINS * LEV * n, 2 * BINS * LEV) for n in range(BLK * TYPES // 2)]
    pairs = [(sources[0].at[rows], kept[0].at[rows]) for rows in pieces]
    pairs += list(zip(sources[1:], kept[1:]))
    copies = [pltpu.make_async_copy(*pair, sems.at[n]) for n, pair in enumerate(pairs)]
    for n in (4, 5, 6, 0, 1, 2, 3, 7, 8, 9):
        copies[n].start()
    wanted = pair_of_column(iota((1, KDIM), 1))
    for first in range(0, KDIM, COLS):
        rows = iota((COLS, KDIM), 0) + first
        chosen[first : first + COLS, :] = jnp.where(rows == wanted, 1.0, 0.0).astype(BF16)
    spec, sat, wind, cloudy = kept[:4]
    for copy in copies[4:7]:
        copy.wait()
    lane = iota((1, COLS), 1)
    owner = ((lane + 2) & 127) >> 2
    row8 = iota((8, COLS), 0)
    main = [jnp.zeros((8, COLS), F32) for _ in range(4)]
    last = jnp.zeros((8, COLS), F32)
    extras = [
        jnp.where(
            row8 == 1,
            sat[n : n + 1, :],
            jnp.where(row8 == 2, wind[n : n + 1, :], cloudy[n // LEV : n // LEV + 1, :].astype(F32)),
        )
        for n in range(BLK * LEV)
    ]
    for b in range(BLK):
        for t in range(TYPES):
            if t & 1 == 0:
                copies[(b * TYPES + t) // 2].wait()
            for l in range(LEV):
                spot = (t * BLK + b) * LEV + l
                mine = owner == spot
                start = block_row(t, b) + l
                for q in range(4):
                    piece = spec[pl.ds(start + 32 * q, 8, stride=LEV), :]
                    main[q] = jnp.where(mine, pltpu.roll(piece, 4 * spot, 1), main[q])
                piece = jnp.where(row8 == 0, spec[start + 128 : start + 129, :], extras[b * LEV + l])
                last = jnp.where(mine, pltpu.roll(piece, 4 * spot, 1), last)
    for q in range(4):
        edge[8 * q : 8 * q + 8, :] = main[q]
    edge[32:40, :] = last
    for copy in copies[7:]:
        copy.wait()


def weights(left, right):
    left_abs = jnp.abs(left)
    right_abs = jnp.abs(right)
    return (
        left_abs - left,
        (right - right_abs) + (7.0 * left - 3.0 * left_abs),
        1.0 - (7.0 * right - 3.0 * right_abs) + (7.0 * left + 3.0 * left_abs),
        -(7.0 * right + 3.0 * right_abs) - (left + left_abs),
        right + right_abs,
    )


def prepare(coll, growth, fall, wind, chosen, lhs, coef, stencil, raw, parts):
    stacked = jnp.concatenate(
        [
            jnp.concatenate([growth[...], fall[...]], axis=0),
            jnp.zeros((COLS - 2 * TYPES, BINS), F32),
        ],
        axis=0,
    )
    stacked = jnp.concatenate([stacked, jnp.zeros((COLS, COLS - BINS), F32)], axis=1)
    turned = jnp.transpose(stacked)[0:40, :]
    for n in range(2 * TYPES):
        coef[n] = jnp.broadcast_to(turned[:, n : n + 1], (40, COLS))
    lane = iota((1, COLS), 1)
    own = wind[...]
    left = jnp.where(lane == 0, 0.0, (own + pltpu.roll(own, 1, 1)) * SCALE)
    right = jnp.where(lane == COLS - 1, 0.0, (own + pltpu.roll(own, COLS - 1, 1)) * SCALE)
    for by, value in zip(range(-2, 3), weights(left, right)):
        inside = (lane + by >= 0) & (lane + by < COLS)
        stencil[by + 2] = jnp.where(inside, value, 0.0)
    raw[KDIM // COLS - 1] = jnp.zeros(raw.shape[1:], F32)
    for n in range(KDIM // COLS):
        width = min(COLS, PAIRS - COLS * n)
        for k in range(BINS):
            raw[n, TYPES * k : TYPES * k + TYPES, 0:width] = coll[k, :, COLS * n : COLS * n + width]
    for t in range(TYPES):
        for n in range(KDIM // COLS):
            rows = raw[n, pl.ds(t, 40, stride=TYPES), :]
            both = jnp.concatenate(split(rows), axis=0)
            parts[MROWS * t : MROWS * t + MROWS, COLS * n : COLS * n + COLS] = both
    lhs[...] = jnp.dot(parts[...], chosen[...], preferred_element_type=F32).astype(BF16)


def condense(main, top, sat, rate_main, rate_top):
    rising = jnp.maximum(sat, 0.0)
    falling = jnp.maximum(-sat, 0.0)
    transfer = rate_main * main
    up = rising * transfer
    down = falling * transfer
    down_top = falling * (rate_top * top)
    arrive_up = jnp.concatenate([jnp.zeros_like(top), up[:-1]], axis=0)
    arrive_down = jnp.concatenate([down[1:], down_top], axis=0)
    new_main = main - up - down + arrive_up + arrive_down
    new_top = top - down_top + up[-1:]
    return new_main, new_top


def pair_parts(groups, turns):
    for (main, top), turn in zip(groups, turns):
        turn[0:32, :] = main
        turn[32:48, :] = main[0:16]

    def gather(pieces):
        return jnp.concatenate(pieces, axis=1) if len(pieces) > 1 else pieces[0]

    for first in range(0, 16, 4):
        tiles = []
        for (main, _), turn in zip(groups, turns):
            parts = [
                split(main * (main if d == 0 else turn[d : d + 32, :]))
                for d in range(first, first + 4)
            ]
            tiles.append(jnp.concatenate([p[0] for p in parts] + [p[1] for p in parts], axis=0))
        columns = slice(32 * first, 32 * first + 128)
        yield (columns, columns), gather(tiles)
    tails = []
    for main, top in groups:
        square = jnp.where(iota((16, COLS), 0) == 0, top * top, 0.0)
        rest = jnp.concatenate([main[0:16] * main[16:32], main * top, square], axis=0)
        tails.append(jnp.concatenate(split(rest), axis=0))
    yield (slice(HALF, KDIM),), gather(tails)


def collect(lhs, groups, turns):
    total = None
    for columns, part in pair_parts(groups, turns):
        gain = jnp.dot(
            jnp.concatenate([lhs[:, c] for c in columns], axis=1), part, preferred_element_type=F32
        )
        total = gain if total is None else total + gain
    return total


def collect_apart(lhs, main, top, turn):
    turn[0:32, :] = main
    turn[32:48, :] = main[0:16]
    total = None
    for first in range(0, 16, 8):
        value = jnp.concatenate(
            [main * (main if d == 0 else turn[d : d + 32, :]) for d in range(first, first + 8)],
            axis=0,
        )
        part = jnp.concatenate(split(value), axis=1)
        gain = jnp.dot(lhs[:, 32 * first : 32 * first + 256], part, preferred_element_type=F32)
        total = gain if total is None else total + gain
    square = jnp.where(iota((16, COLS), 0) == 0, top * top, 0.0)
    rest = jnp.concatenate([main[0:16] * main[16:32], main * top, square], axis=0)
    part = jnp.concatenate(split(rest), axis=1)
    total = total + jnp.dot(lhs[:, HALF : HALF + TAIL], part, preferred_element_type=F32)
    return total[:, 0:COLS] + total[:, COLS : 2 * COLS]


UP = ((6, 4, 3, 1, 0, 0, 0, 0), (6, 5, 4, 2, 1, 1, 1, 0))
DOWN = ((7, 5, 4, 2, 1, 1, 1, 0), (6, 5, 4, 2, 1, 1, 1, 0))


def shares():
    x, y = lax.axis_index("gx"), lax.axis_index("gy")

    def pick(table):
        value = jnp.int32(0)
        for odd in range(2):
            for z, count in enumerate(table[odd]):
                value = jnp.where(y == 2 * z + odd, count, value)
        return value

    first, second = pick(UP), pick(DOWN)
    for n, pair in enumerate(((0, 1), (6, 6), (1, 2), (4, 5))):
        special = (x == 0) & (y == n)
        first = jnp.where(special, pair[0], first)
        second = jnp.where(special, pair[1], second)
    return (0, first), (first, second), (second, BLK * TYPES)


def main_kernel(which, spec, sat, wind, cloudy, coll, growth, fall, chosen, edge, *rest):
    result, rim, lhs, coef, stencil = rest[-10:-5] if which < 2 else rest[-9:-4]
    turn, raw, parts, held = rest[-4:]
    if which < 2:
        rest[-5][...] = edge[...]
    begin, end = shares()[which]
    owner = ((iota((1, COLS), 1) + 2) & (COLS - 1)) >> 2

    @pl.when((begin == 0) & (end > 0))
    def _():
        prepare(coll, growth, fall, wind, chosen, lhs, coef, stencil, raw, parts)

    def advect(n):
        t = n >> 1
        b = n & 1
        start = block_row(t, b)
        for l in range(LEV):
            settled = held[l]
            spot = n * LEV + l
            rim[...] = jnp.where(owner == spot, pltpu.roll(settled, 4 * spot, 1), rim[...])
            w = [stencil[k, pl.ds(b * LEV + l, 1), :] for k in range(5)]
            y = w[2] * settled
            for by in (-2, -1, 1, 2):
                y = y + w[by + 2] * pltpu.roll(settled, (COLS - by) % COLS, 1)
            for q in range(4):
                result[pl.ds(start + l + 32 * q, 8, stride=LEV), :] = y[8 * q : 8 * q + 8]
            result[pl.ds(start + l + 128, 1), :] = y[32:33]

    def one(n, carry):
        advect(jnp.maximum(n - 1, begin))
        t = n >> 1
        b = n & 1
        start = block_row(t, b)
        left = lhs[pl.ds(pl.multiple_of(t * MROWS, 16), MROWS), :]
        rate = coef[t]
        speed = coef[TYPES + t]
        wet = cloudy[pl.ds(b, 1), :] > 0
        before = []
        state = []
        for l in range(LEV):
            main = spec[pl.ds(start + l, 32, stride=LEV), :]
            top = spec[pl.ds(start + 128 + l, 1), :]
            before.append((main, top))
            row = sat[pl.ds(b * LEV + l, 1), :]
            state.append(condense(main, top, row, rate[0:32], rate[32:33]))
        for step in range(SUB):
            for half in range(2):
                levels = range(2 * half, 2 * half + 2)
                gain = collect(
                    left,
                    [state[l] for l in levels],
                    [turn.at[LEV * step + l] for l in levels],
                )
                for k in range(2):
                    l = 2 * half + k
                    mine = gain[:, COLS * k : COLS * k + COLS]
                    main, top = state[l]
                    state[l] = (
                        main + (mine[0:32] + mine[40:72]),
                        top + (mine[32:33] + mine[72:73]),
                    )
        above = None
        for l in reversed(range(LEV)):
            main = jnp.where(wet, state[l][0], before[l][0])
            top = jnp.where(wet, state[l][1], before[l][1])
            over = (jnp.zeros_like(main), jnp.zeros_like(top)) if above is None else above
            held[l, 0:32, :] = main + speed[0:32] * (over[0] - main)
            held[l, 32:40, :] = jnp.broadcast_to(top + speed[32:33] * (over[1] - top), (8, COLS))
            above = (main, top)
        return carry

    lax.fori_loop(begin, end, one, 0)

    @pl.when(end > begin)
    def _():
        advect(end - 1)


def finish_kernel(result, rim, from_left, from_right, edge, lhs, coef, out, turn, final, sems):
    lane = iota((1, COLS), 1)
    owner = ((lane + 2) & 127) >> 2
    kind = owner >> 3
    place = lane & 3
    halo = jnp.where(place < 2, from_right[...], from_left[...])

    def by_type(pieces):
        value = pieces[0]
        for t in range(1, TYPES):
            value = jnp.where(kind == t, pieces[t], value)
        return value

    rate = by_type([coef[t] for t in range(TYPES)])
    speed = by_type([coef[TYPES + t] for t in range(TYPES)])
    main = halo[0:32]
    top = halo[32:33]
    wet = halo[35:36] > 0
    state = condense(main, top, halo[33:34], rate[0:32], rate[32:33])
    for step in range(SUB):
        gain = collect_apart(lhs, *state, turn.at[step])
        share = by_type([gain[MROWS * t : MROWS * t + MROWS] for t in range(TYPES)])
        state = (
            state[0] + (share[0:32] + share[40:72]),
            state[1] + (share[32:33] + share[72:73]),
        )
    highest = (owner & 3) == LEV - 1

    def settle(value, speed):
        above = jnp.where(highest, 0.0, pltpu.roll(value, COLS - 4, 1))
        return value + speed * (above - value)

    ghost = jnp.concatenate(
        [
            settle(jnp.where(wet, state[0], main), speed[0:32]),
            settle(jnp.broadcast_to(jnp.where(wet, state[1], top), (8, COLS)), speed[32:40]),
        ],
        axis=0,
    )

    far = jnp.broadcast_to(halo[34:35], (8, COLS))
    near = jnp.broadcast_to(edge[34:35], (8, COLS))
    lower = jnp.where(place == 0, pltpu.roll(far, 1, 1), pltpu.roll(near, 1, 1))
    upper = jnp.where(place == 3, pltpu.roll(far, COLS - 1, 1), pltpu.roll(near, COLS - 1, 1))
    left = (near + lower) * SCALE
    right = (near + upper) * SCALE
    left_abs = jnp.abs(left)
    right_abs = jnp.abs(right)

    def by_place(first, second, third, fourth):
        value = jnp.where(place == 0, first, jnp.where(place == 3, fourth, 0.0))
        return jnp.where(place == 1, second, jnp.where(place == 2, third, value))[0:1]

    own_0 = by_place(7.0 * left + 3.0 * left_abs, 0.0, 0.0, -(7.0 * right - 3.0 * right_abs))
    own_1 = by_place(-(left + left_abs), 0.0, 0.0, right - right_abs)
    halo_1 = by_place(
        (7.0 * left - 3.0 * left_abs) + (right - right_abs),
        0.0,
        0.0,
        -(7.0 * right + 3.0 * right_abs) - (left + left_abs),
    )
    halo_2 = by_place(
        left_abs - left, left_abs - left, right + right_abs, right + right_abs
    )
    inner = rim[...]
    inner_1 = jnp.where(place == 0, pltpu.roll(inner, COLS - 1, 1), pltpu.roll(inner, 1, 1))
    ghost_1 = jnp.where(place == 0, pltpu.roll(ghost, 1, 1), pltpu.roll(ghost, COLS - 1, 1))
    ghost_2 = jnp.where(place < 2, pltpu.roll(ghost, 2, 1), pltpu.roll(ghost, COLS - 2, 1))
    extra = own_0 * inner + own_1 * inner_1 + halo_1 * ghost_1 + halo_2 * ghost_2

    outer = (lane < 2) | (lane >= COLS - 2)
    pieces = [pl.ds(2 * BINS * LEV * n, 2 * BINS * LEV) for n in range(BLK * TYPES // 2)]
    copies = [
        pltpu.make_async_copy(final.at[rows], out.at[rows], sems.at[n])
        for n, rows in enumerate(pieces)
    ]
    for b in range(BLK):
        for t in range(TYPES):
            for l in range(LEV):
                spot = (t * BLK + b) * LEV + l
                added = jnp.where(outer, pltpu.roll(extra, (COLS - 4 * spot) % COLS, 1), 0.0)
                start = block_row(t, b) + l
                for q in range(4):
                    rows = pl.ds(start + 32 * q, 8, stride=LEV)
                    final[rows, :] = result[rows, :] + added[8 * q : 8 * q + 8]
                rows = slice(start + 128, start + 129)
                final[rows, :] = result[rows, :] + added[32:33]
            if t & 1:
                copies[(b * TYPES + t) // 2].start()
    for copy in copies:
        copy.wait()


def vmem(count):
    return [pl.BlockSpec(memory_space=pltpu.VMEM)] * count


def placed(space, *arrays):
    return [pltpu.with_memory_space_constraint(x, space) for x in arrays]


def resident(*arrays):
    return placed(pltpu.VMEM, *arrays)


def body(spectra, collection, growth_rate, fall_speed, supersaturation, courant, cloudy):
    sources = (
        spectra.reshape(ROWS, COLS),
        supersaturation.reshape(BLK * LEV, COLS),
        courant.reshape(BLK * LEV, COLS),
        cloudy,
        jnp.transpose(collection, (1, 0, 2)),
        growth_rate,
        fall_speed,
    )
    edge, chosen, spec, sat, wind, wet, coll, growth, fall = pl.pallas_call(
        edge_kernel,
        out_shape=(
            pltpu.VMEM((40, COLS), F32),
            pltpu.VMEM((KDIM, KDIM), BF16),
            *(pltpu.VMEM(x.shape, x.dtype) for x in sources),
        ),
        in_specs=[pl.BlockSpec(memory_space=pltpu.HBM)] * len(sources),
        out_specs=tuple(vmem(2 + len(sources))),
        scratch_shapes=[pltpu.SemaphoreType.DMA((3 + len(sources),))],
        compiler_params=pltpu.CompilerParams(vmem_limit_bytes=LIMIT),
        name="edges",
    )(*placed(pltpu.HBM, *sources))

    def blocks(which, edge, held):
        shapes = (
            pltpu.VMEM((ROWS, COLS), F32),
            pltpu.VMEM((40, COLS), F32),
            pltpu.VMEM((TYPES * MROWS, KDIM), BF16),
            pltpu.VMEM((2 * TYPES, 40, COLS), F32),
            pltpu.VMEM((5, BLK * LEV, COLS), F32),
        )
        if which < 2:
            shapes += (pltpu.VMEM((40, COLS), F32),)
        return pl.pallas_call(
            lambda *refs: main_kernel(which, *refs),
            out_shape=shapes,
            in_specs=vmem(9 + len(held)),
            out_specs=tuple(vmem(len(shapes))),
            input_output_aliases={9 + n: n for n in range(len(held))},
            scratch_shapes=[
                pltpu.VMEM((SUB * LEV, 48, COLS), F32),
                pltpu.VMEM((KDIM // COLS, TYPES * 40, COLS), F32),
                pltpu.VMEM((TYPES * MROWS, KDIM), BF16),
                pltpu.VMEM((LEV, 40, COLS), F32),
            ],
            compiler_params=pltpu.CompilerParams(vmem_limit_bytes=LIMIT),
        )(*resident(spec, sat, wind, wet, coll, growth, fall, chosen, edge, *held))

    count = lax.axis_size("gy")
    up = [(i, (i + 1) % count) for i in range(count)]
    down = [(j, i) for i, j in up]
    *held, edge0 = blocks(0, edge, ())
    from_left = lax.ppermute(edge0, "gy", up)
    *held, edge1 = blocks(1, edge0, held)
    from_right = lax.ppermute(edge1, "gy", down)
    result, rim, lhs, coef, _ = blocks(2, edge1, held)
    out = pl.pallas_call(
        finish_kernel,
        out_shape=jax.ShapeDtypeStruct((ROWS, COLS), F32),
        in_specs=vmem(7),
        out_specs=pl.BlockSpec(memory_space=pl.ANY),
        scratch_shapes=[
            pltpu.VMEM((SUB, 48, COLS), F32),
            pltpu.VMEM((ROWS, COLS), F32),
            pltpu.SemaphoreType.DMA((BLK * TYPES // 2,)),
        ],
        compiler_params=pltpu.CompilerParams(vmem_limit_bytes=LIMIT),
        name="finish",
    )(*resident(result, rim, from_left, from_right, edge, lhs, coef))
    return out.reshape(spectra.shape)


def solution(mesh):
    return jax.shard_map(
        body,
        mesh=mesh,
        in_specs=(
            P("gx", None, None, None, "gy"),
            P(),
            P(),
            P(),
            P("gx", None, "gy"),
            P("gx", None, "gy"),
            P("gx", "gy"),
        ),
        out_specs=P("gx", None, None, None, "gy"),
        check_vma=False,
    )
```
